256 devices in a mesh: section: 16 (over z_lo, y), ctx: 4 (over x), tensor: 4 (over z_hi, core).
Axes of the slice: x: 4, y: 4, z: 8 (z_hi: 2, z_lo: 4; z = z_hi * 4 + z_lo), core: 2. Of those that a mesh axis runs over, the one named last changes fastest.
Arguments:
- arriving: bfloat16 [16, 1024, 4096], P('section', 'ctx', 'tensor')
- stored: bfloat16 [16, 1024, 4096], P('section', 'ctx', 'tensor')
- docs_forward: int32 [16, 1024], P('section', 'ctx'), may hold values from 0 to 3, never falling along the last dimension, each value on 1 to 512 neighbouring positions
- docs_backward: int32 [16, 1024], P('section', 'ctx'), may hold values from 0 to 3, never falling along the last dimension, each value on 1 to 512 neighbouring positions
- norm_gain: bfloat16 [16, 4096], P('section')
- query_weight: bfloat16 [16, 4096, 4096], P('section', 'ctx', 'tensor')
- key_weight: bfloat16 [16, 4096, 512], P('section', 'ctx', 'tensor')
- value_projection_weight: bfloat16 [16, 4096, 512], P('section', 'ctx', 'tensor'), may hold values from -0.09375 to 0.09375
- out_weight: bfloat16 [16, 4096, 4096], P('section', 'tensor', 'ctx'), may hold values from -0.375 to 0.375
Outputs:
- forward_output: bfloat16 [16, 1024, 4096], P('section', 'ctx', 'tensor')
- stashed: bfloat16 [16, 1024, 4096], P('section', 'ctx', 'tensor')
- rebuilt: bfloat16 [16, 1024, 4096], P('section', 'ctx', 'tensor')
The draws below stay inside these ranges and needn't reach their ends.
Inputs may be any that keep to these rules, and one draw needn't show every extreme that they name: `docs_forward`: each row holds 4 packed documents: ids never fall, each document has 1 to 512 tokens, one exactly 512. `docs_backward`: each row holds 4 packed documents: ids never fall, each document has 1 to 512 tokens, one exactly 512.
All inputs are finite; a program needn't handle non-finite values.
Results may differ from the reference program's by a relative error of at most 0.0066.
Values may be sent and summed in bfloat16 or wider, within the bound.
No kernel may reach another device: no remote copies, remote signals or barrier semaphores. Data moves between devices by JAX's collectives and lax.ppermute only.
A program may use at most 128 MiB of HBM per device.

```python
import math
import jax
import jax.numpy as jnp
import numpy as np
from jax import lax

MODEL_WIDTH = 4096
HEAD = 128
QH = 32
KVH = 4
DOCS = 4
HQ = 4096
KEY_FEATURES = 512
SEQ = 1024
RELAY_SECTIONS = 16
DOC_MOST = 512


def activation_draw(base_key):
    keys_list = jax.random.split(base_key, 3)
    shape_full = (RELAY_SECTIONS, SEQ, MODEL_WIDTH)
    noise_values = jnp.clip(jax.random.normal(keys_list[0], shape_full, jnp.float32), -4.0, 4.0)
    row_scale = jnp.exp(jax.random.uniform(keys_list[1], (RELAY_SECTIONS, SEQ, 1), jnp.float32, math.log(0.5), math.log(2.0)))
    column_scale = jnp.exp(jax.random.uniform(keys_list[2], (1, 1, MODEL_WIDTH), jnp.float32, math.log(0.7), math.log(1.4)))
    return (noise_values * row_scale * column_scale).astype(jnp.bfloat16)


def draw_arriving(key, part):
    return activation_draw(jax.random.fold_in(key, 1))


def draw_stored(key, part):
    return activation_draw(jax.random.fold_in(key, 2))


def draw_norm_gain(key, part):
    gain_key = jax.random.fold_in(key, 3)
    return jax.random.uniform(gain_key, (RELAY_SECTIONS, MODEL_WIDTH), jnp.float32, 0.6, 1.6).astype(jnp.bfloat16)


def key_base(key):
    noise_values = jnp.clip(jax.random.normal(jax.random.fold_in(key, 31), (RELAY_SECTIONS, MODEL_WIDTH, KVH * HEAD), jnp.float32), -4.0, 4.0)
    return noise_values * (1.0 / math.sqrt(MODEL_WIDTH))


def draw_key_weight(key, part):
    return key_base(key).astype(jnp.bfloat16)


def draw_query_weight(key, part):
    noise_values = jnp.clip(jax.random.normal(jax.random.fold_in(key, 32), (RELAY_SECTIONS, MODEL_WIDTH, QH * HEAD), jnp.float32), -4.0, 4.0) * (1.0 / math.sqrt(MODEL_WIDTH))
    return noise_values.astype(jnp.bfloat16)


def shard_levels(stream_key, extent, pieces, smallest, largest):
    def one(axis_at, parts):
        heights = jax.random.uniform(jax.random.fold_in(jax.random.fold_in(stream_key, 6), axis_at), (parts,), jnp.float32, smallest / len(pieces), largest / len(pieces))
        return jnp.repeat(jnp.exp(heights), extent[axis_at] // parts).reshape((-1,) + (1,) * (len(extent) - axis_at - 1))

    factor_of = one(*pieces[0])
    for cut in pieces[1:]:
        factor_of = factor_of * one(*cut)
    return factor_of


def split_up(count, total, limit, skew):
    loads = [(1 << 20) // math.isqrt(standing ** skew) + 1 for standing in range(2, count + 1)]
    surplus, given = total - limit - (count - 1), [1] * (count - 1)
    while surplus > 0:
        candidates = [i for i in range(count - 1) if given[i] < limit]
        mass, remaining = sum([loads[i] for i in candidates]), surplus
        for i in candidates:
            addition = min(limit - given[i], max(1, remaining * loads[i] // mass), surplus)
            given[i] = given[i] + addition
            surplus = surplus - addition
    return np.array([limit] + given)


def ragged(key, amount, total, limit, skew):
    if amount == 2:
        one = jax.random.randint(key, (), max(1, total - limit), min(limit, total - 1) + 1)
        return jnp.stack([one, total - one])
    lengths = jnp.asarray(split_up(amount, total, limit, skew), jnp.int32)
    twos = (amount - 1) // 2
    donor, sink = lengths[1:1 + 2 * twos:2], lengths[2:2 + 2 * twos:2]
    slack = jnp.minimum(donor - 1, limit - sink)
    shifted = jax.random.randint(jax.random.fold_in(key, 1), (twos,), 0, 1 << 20) % (slack + 1)
    lengths = lengths.at[1:1 + 2 * twos:2].set(donor - shifted).at[2:2 + 2 * twos:2].set(sink + shifted)
    return lengths[jax.random.permutation(jax.random.fold_in(key, 2), amount)]


def scatter_about(key, shape, deviation, limit, shards=(), kind=jnp.bfloat16):
    array = deviation * jax.random.normal(key, shape, jnp.float32)
    if shards:
        array = array * shard_levels(key, shape, shards, -0.22, 0.18)
    return jnp.clip(array, -limit, limit).astype(kind)


def setup_inputs(seed: int = 0) -> dict:
    streams_of = jax.random.split(jax.random.key(seed), 10)
    arriving = draw_arriving(jax.random.fold_in(streams_of[9], 71), 0)
    stored = draw_stored(jax.random.fold_in(streams_of[9], 71), 0)
    docs_forward = jax.vmap(lambda own: jnp.searchsorted(jnp.cumsum(ragged(own, DOCS, SEQ, DOC_MOST, 2)), jnp.arange(SEQ), side="right"))(jax.random.split(streams_of[2], RELAY_SECTIONS)).reshape((RELAY_SECTIONS, SEQ)).astype(jnp.int32)
    docs_backward = jax.vmap(lambda own: jnp.searchsorted(jnp.cumsum(ragged(own, DOCS, SEQ, DOC_MOST, 2)), jnp.arange(SEQ), side="right"))(jax.random.split(streams_of[3], RELAY_SECTIONS)).reshape((RELAY_SECTIONS, SEQ)).astype(jnp.int32)
    norm_gain = draw_norm_gain(jax.random.fold_in(streams_of[9], 71), 0)
    query_weight = draw_query_weight(jax.random.fold_in(streams_of[9], 71), 0)
    key_weight = draw_key_weight(jax.random.fold_in(streams_of[9], 71), 0)
    value_projection_weight = scatter_about(streams_of[7], (RELAY_SECTIONS, MODEL_WIDTH, KEY_FEATURES), MODEL_WIDTH ** -0.5, 0.09375, ((0, 16), (1, 4), (2, 4)))
    out_weight = scatter_about(streams_of[8], (RELAY_SECTIONS, HQ, MODEL_WIDTH), (HQ // 16) ** -0.5, 0.375, ((0, 16), (1, 4), (2, 4)))
    return {"arriving": arriving, "stored": stored, "docs_forward": docs_forward, "docs_backward": docs_backward, "norm_gain": norm_gain, "query_weight": query_weight, "key_weight": key_weight, "value_projection_weight": value_projection_weight, "out_weight": out_weight}


norm_epsilon = 1e-05
rope_base = 500000.0

def normalize(inputs, gain_row):
    values = inputs.astype(jnp.float32)
    mean_square = lax.optimization_barrier(jnp.mean(values * values, axis=-1, keepdims=True))
    return (values * lax.rsqrt(mean_square + norm_epsilon) * gain_row.astype(jnp.float32)).astype(jnp.bfloat16)

def rotary(values, positions, head_size):
    half_size = head_size // 2
    tokens = values.shape[0]
    shaped = values.reshape(tokens, -1, head_size)
    exponent = jnp.arange(half_size).astype(jnp.float32) * (2.0 / head_size)
    inverse = jnp.exp(-exponent * math.log(rope_base))
    angles = positions.astype(jnp.float32)[:, None] * inverse[None, :]
    cosine_lookup = jnp.cos(angles)[:, None, :]
    sine_table = jnp.sin(angles)[:, None, :]
    first_half = shaped[:, :, :half_size]
    second_half = shaped[:, :, half_size:]
    turned = jnp.concatenate((first_half * cosine_lookup - second_half * sine_table, second_half * cosine_lookup + first_half * sine_table), axis=2)
    return turned.reshape(tokens, -1)

def attend(queries, key_rows, value_rows, positions, doc_ids):
    token_count = queries.shape[0]
    group_count = key_rows.shape[1] // HEAD
    group_size = QH // KVH
    permitted_mask = (positions[None, :] <= positions[:, None]) & (doc_ids[None, :] == doc_ids[:, None])
    grouped = queries.reshape(token_count, group_count, group_size, HEAD).astype(jnp.float32)
    key_heads = key_rows.reshape(token_count, group_count, HEAD).astype(jnp.float32)
    value_heads = value_rows.reshape(token_count, group_count, HEAD).astype(jnp.float32)

    def one_group(operands):
        group_queries, group_keys, group_values = operands
        scores = jnp.einsum('qgh,sh->gqs', group_queries, group_keys) * (1.0 / math.sqrt(HEAD))
        masked = jnp.where(permitted_mask[None], scores, -jnp.inf)
        row_peak = lax.optimization_barrier(jnp.max(masked, axis=2, keepdims=True))
        weights = jnp.exp(masked - row_peak)
        totals = lax.optimization_barrier(jnp.sum(weights, axis=2, keepdims=True))
        probabilities = weights.astype(jnp.bfloat16).astype(jnp.float32)
        mixed_heads = jnp.einsum('gqs,sh->gqh', probabilities, group_values) / totals
        return mixed_heads
    outputs = lax.map(one_group, (jnp.transpose(grouped, (1, 0, 2, 3)), jnp.transpose(key_heads, (1, 0, 2)), jnp.transpose(value_heads, (1, 0, 2))))
    return jnp.transpose(outputs, (2, 0, 1, 3)).reshape(token_count, -1).astype(jnp.bfloat16)

def apply_layer(operands):
    inputs, doc_ids, gain_row, query_matrix, key_matrix, value_matrix, out_matrix = operands
    normed = normalize(inputs, gain_row)
    positions = jnp.arange(SEQ).astype(jnp.int32)
    queries = rotary(jnp.dot(normed, query_matrix, preferred_element_type=jnp.float32), positions, HEAD).astype(jnp.bfloat16)
    key_rows = rotary(jnp.dot(normed, key_matrix, preferred_element_type=jnp.float32), positions, HEAD).astype(jnp.bfloat16)
    value_rows = jnp.dot(normed, value_matrix, preferred_element_type=jnp.float32).astype(jnp.bfloat16)
    mixed_heads = attend(queries, key_rows, value_rows, positions, doc_ids)
    summed = jnp.dot(mixed_heads, out_matrix, preferred_element_type=jnp.float32)
    return (inputs.astype(jnp.float32) + summed).astype(jnp.bfloat16)

def reference(arriving, stored, docs_forward, docs_backward, norm_gain, query_weight, key_weight, value_projection_weight, out_weight):
    forward_output = lax.map(apply_layer, (arriving, docs_forward, norm_gain, query_weight, key_weight, value_projection_weight, out_weight))
    stashed = jnp.roll(arriving, RELAY_SECTIONS // 2, axis=0)
    fetched = jnp.roll(stored, RELAY_SECTIONS // 2, axis=0)
    rebuilt = lax.map(apply_layer, (fetched, docs_backward, norm_gain, query_weight, key_weight, value_projection_weight, out_weight))
    return (forward_output, stashed, rebuilt)
```

```python
import functools
import math

import jax
import jax.numpy as jnp
from jax import lax
from jax.experimental import pallas as pl
from jax.experimental.pallas import tpu as pltpu
from jax.sharding import PartitionSpec as P

HEAD = 128
norm_epsilon = 1e-05
rope_base = 500000.0
BF = jnp.bfloat16
F32 = jnp.float32
OUT_CHUNKS = 4


def after(value, *earlier):
    return lax.optimization_barrier((value,) + earlier)[0]


def z_route(step, sections, tensors):
    low_count = 4
    rows = sections // low_count
    cores = 2
    high_count = tensors // cores
    depth = low_count * high_count
    route = []
    for z in range(depth):
        origin = (z + step) % depth
        for y in range(rows):
            for core in range(cores):
                source = ((origin % low_count) * rows + y) * tensors + (origin // low_count) * cores + core
                target = ((z % low_count) * rows + y) * tensors + (z // low_count) * cores + core
                route.append((source, target))
    return route


def from_z(block, step):
    route = z_route(step, lax.axis_size("section"), lax.axis_size("tensor"))
    return lax.ppermute(block, ("section", "tensor"), route)


def from_x(block, step):
    count = lax.axis_size("ctx")
    return lax.ppermute(block, "ctx", [((c + step) % count, c) for c in range(count)])


def from_before(block, step):
    count = lax.axis_size("ctx")
    return lax.ppermute(block, "ctx", [(c - step, c) for c in range(step, count)])


def from_tensor(block, flip):
    count = lax.axis_size("tensor")
    return lax.ppermute(block, "tensor", [(t, t ^ flip) for t in range(count)])


def first_hop(shard):
    return from_x(shard, 1), from_x(shard, -1)


def second_hop(ahead, behind):
    half = ahead.shape[0] // 2
    return from_x(ahead[:half], 1), from_x(behind[half:], -1)


def rope_tables(rows):
    half = HEAD // 2
    exponent = jnp.arange(half).astype(F32) * (2.0 / HEAD)
    inverse = jnp.exp(-exponent * math.log(rope_base))
    positions = lax.axis_index("ctx") * rows + jnp.arange(rows, dtype=jnp.int32)
    angles = positions.astype(F32)[:, None] * inverse[None, :]
    cosine = jnp.cos(angles)
    sine = jnp.sin(angles)
    return jnp.concatenate((cosine, cosine), axis=1), jnp.concatenate((-sine, sine), axis=1)


def attend_kernel(query_ref, cosine_ref, sine_ref, key_ref, value_ref, query_doc_ref, key_doc_ref, out_ref, bias_ref):
    rows, span = bias_ref.shape
    back = span - rows

    @pl.when(pl.program_id(1) == 0)
    def _():
        at_query = lax.broadcasted_iota(jnp.int32, (rows, span), 0)
        at_key = lax.broadcasted_iota(jnp.int32, (rows, span), 1) - back
        allowed = (at_key <= at_query) & (query_doc_ref[0] == key_doc_ref[0])
        bias_ref[...] = jnp.where(allowed, 0.0, -jnp.inf)

    raw = query_ref[...]
    turned = raw * cosine_ref[...] + pltpu.roll(raw, HEAD // 2, 1) * sine_ref[...]
    queries = turned.astype(BF)
    scores = lax.dot_general(queries, key_ref[0], (((1,), (1,)), ((), ())), preferred_element_type=F32)
    masked = scores + bias_ref[...]
    peak = jnp.max(masked, axis=1, keepdims=True)
    weights = jnp.exp((masked - peak) * (1.0 / math.sqrt(HEAD)))
    totals = jnp.sum(weights, axis=1, keepdims=True)
    mixed = jnp.dot(weights.astype(BF), value_ref[0], preferred_element_type=F32)
    out_ref[...] = (mixed / totals).astype(BF)


def attend(query_raw, cosine, sine, keys, values, query_docs, key_docs):
    batches, span, _ = keys.shape
    rows = query_raw.shape[0] // batches
    heads = query_raw.shape[1] // HEAD
    return pl.pallas_call(
        attend_kernel,
        grid=(batches, heads),
        in_specs=[
            pl.BlockSpec((rows, HEAD), lambda b, h: (b, h)),
            pl.BlockSpec((rows, HEAD), lambda b, h: (0, 0)),
            pl.BlockSpec((rows, HEAD), lambda b, h: (0, 0)),
            pl.BlockSpec((1, span, HEAD), lambda b, h: (b, 0, 0)),
            pl.BlockSpec((1, span, HEAD), lambda b, h: (b, 0, 0)),
            pl.BlockSpec((1, rows, 1), lambda b, h: (b, 0, 0)),
            pl.BlockSpec((1, 1, span), lambda b, h: (b, 0, 0)),
        ],
        out_specs=pl.BlockSpec((rows, HEAD), lambda b, h: (b, h)),
        out_shape=jax.ShapeDtypeStruct(query_raw.shape, BF),
        scratch_shapes=[pltpu.VMEM((rows, span), F32)],
        compiler_params=pltpu.CompilerParams(vmem_limit_bytes=24 << 20),
        cost_estimate=pl.CostEstimate(
            flops=4 * batches * heads * rows * span * HEAD,
            transcendentals=batches * heads * rows * span,
            bytes_accessed=6 * query_raw.size,
        ),
        name="attend",
    )(query_raw, cosine, sine, keys, values, query_docs, key_docs)


def body(
    arriving,
    stored,
    docs_forward,
    docs_backward,
    norm_gain,
    query_weight,
    key_weight,
    value_projection_weight,
    out_weight,
):
    mine = arriving[0]
    held = stored[0]
    rows, width = mine.shape
    ring = lax.axis_size("ctx")
    c = lax.axis_index("ctx")
    t = lax.axis_index("tensor")
    near_high = lax.axis_index("section") < lax.axis_size("section") // 2
    docs = jnp.stack((docs_forward[0], docs_backward[0]), axis=0)

    kv_weight = jnp.concatenate((key_weight[0], value_projection_weight[0]), axis=1)
    kv_ahead, kv_behind = first_hop(kv_weight)
    docs_one, docs_two = from_before(docs, 1), from_before(docs, 2)
    held_up, held_down = from_z(held, 2), from_z(held, -2)

    kv_far = second_hop(kv_ahead, kv_behind)
    q_weight = query_weight[0]
    q_ahead, q_behind = first_hop(after(q_weight, kv_ahead, kv_behind))

    mine_later = after(mine, held_up, held_down)
    mine_up, mine_down = from_z(mine_later, 2), from_z(mine_later, -2)
    stashed = jnp.where(near_high, mine_up, mine_down)
    fetched = jnp.where(near_high, held_up, held_down)
    fetched_far = jnp.where(near_high, held_down, held_up)
    half = rows // 2
    mine_far = jnp.concatenate((from_z(mine_up[:half], 2), from_z(mine_down[half:], -2)), axis=0)
    fetched_pair = jnp.concatenate((fetched, fetched_far), axis=0)
    fetched_sib = from_tensor(fetched_pair, 1)
    mine_sib = from_tensor(mine, 1)
    mine_far_sib = from_tensor(mine_far, 1)
    forward_blocks = (mine, mine_sib, mine_far, mine_far_sib)
    backward_blocks = (fetched, fetched_sib[:rows], fetched_far, fetched_sib[rows:])

    gains = norm_gain[0].reshape(-1, width)
    gain_blocks = [lax.dynamic_index_in_dim(gains, t ^ j, 0, keepdims=True).astype(F32) for j in range(4)]

    def normalize(blocks):
        total = sum(jnp.sum(jnp.square(b.astype(F32)), axis=1, keepdims=True) for b in blocks)
        scale = lax.rsqrt(total * (1.0 / (width * len(blocks))) + norm_epsilon)
        return [(b.astype(F32) * scale * g).astype(BF) for b, g in zip(blocks, gain_blocks)]

    normed = jnp.stack(
        [
            jnp.concatenate(pair, axis=0)
            for pair in zip(normalize(forward_blocks), normalize(backward_blocks))
        ],
        axis=0,
    )

    def features(step):
        return lax.dynamic_index_in_dim(normed, t ^ ((c + step) % ring), 0, keepdims=False)

    def project(own, ahead, behind, far):
        depth = own.shape[0] // 2
        total = jnp.dot(features(0), own, preferred_element_type=F32)
        total += jnp.dot(features(1), ahead, preferred_element_type=F32)
        total += jnp.dot(features(3), behind, preferred_element_type=F32)
        across = features(2)
        total += jnp.dot(across[:, :depth], far[0], preferred_element_type=F32)
        total += jnp.dot(across[:, depth:], far[1], preferred_element_type=F32)
        return total

    cosine, sine = rope_tables(rows)
    kv_raw = project(kv_weight, kv_ahead, kv_behind, kv_far)
    key_raw = kv_raw[:, :HEAD].reshape(2, rows, HEAD)
    key_swapped = jnp.concatenate((key_raw[:, :, HEAD // 2 :], key_raw[:, :, : HEAD // 2]), axis=2)
    own_keys = (key_raw * cosine[None] + key_swapped * sine[None]).astype(BF)
    own_kv = jnp.concatenate((own_keys, kv_raw[:, HEAD:].reshape(2, rows, HEAD).astype(BF)), axis=2)
    kv_one, kv_two = from_before(own_kv, 1), from_before(own_kv, 2)
    all_kv = jnp.concatenate((kv_two, kv_one, own_kv), axis=1)
    key_docs = jnp.concatenate(
        (jnp.where(c >= 2, docs_two, -1), jnp.where(c >= 1, docs_one, -1), docs), axis=1
    )

    chunk = width // OUT_CHUNKS
    out_own = [out_weight[0][:, i * chunk : (i + 1) * chunk] for i in range(OUT_CHUNKS)]
    out_parts = []
    gate = (q_ahead, q_behind)
    q_far = second_hop(q_ahead, q_behind)
    for piece in out_own:
        ahead, behind = first_hop(after(piece, *gate))
        gate = (ahead, behind)
        out_parts.append((piece, ahead, behind, second_hop(ahead, behind)))

    query_raw = project(q_weight, q_ahead, q_behind, q_far)
    mixed = attend(
        query_raw,
        cosine,
        sine,
        all_kv[:, :, :HEAD],
        all_kv[:, :, HEAD:],
        docs[:, :, None],
        key_docs[:, None, :],
    )

    residual = jnp.concatenate((mine, fetched), axis=0)
    outputs = []
    for index, (own, ahead, behind, far) in enumerate(out_parts):
        across = jnp.concatenate(far, axis=0)
        terms = jnp.stack(
            [jnp.dot(mixed, w, preferred_element_type=F32) for w in (own, ahead, across, behind)], axis=0
        )

        def term(j):
            return lax.dynamic_index_in_dim(terms, ((t ^ j) - c) % ring, 0, keepdims=False)

        sent = jnp.concatenate((term(1).astype(BF), term(3).astype(BF)), axis=0)
        received = from_tensor(sent, 1)
        kept = term(0) + received[: 2 * rows].astype(F32)
        passed = (term(2) + received[2 * rows :].astype(F32)).astype(BF)
        arrived = from_tensor(passed, 2)
        base = residual[:, index * chunk : (index + 1) * chunk].astype(F32)
        outputs.append((base + (kept + arrived.astype(F32))).astype(BF))
    result = jnp.concatenate(outputs, axis=1)
    return (result[:rows][None], stashed[None], result[rows:][None])


def solution(mesh):
    return jax.shard_map(
        body,
        mesh=mesh,
        in_specs=(
            P("section", "ctx", "tensor"),
            P("section", "ctx", "tensor"),
            P("section", "ctx"),
            P("section", "ctx"),
            P("section", None),
            P("section", "ctx", "tensor"),
            P("section", "ctx", "tensor"),
            P("section", "ctx", "tensor"),
            P("section", "tensor", "ctx"),
        ),
        out_specs=(
            P("section", "ctx", "tensor"),
            P("section", "ctx", "tensor"),
            P("section", "ctx", "tensor"),
        ),
        check_vma=False,
    )
```

```python
import functools
import math

import jax
import jax.numpy as jnp
from jax import lax
from jax.experimental import pallas as pl
from jax.experimental.pallas import tpu as pltpu
from jax.sharding import PartitionSpec as P

HEAD = 128
norm_epsilon = 1e-05
rope_base = 500000.0
BF = jnp.bfloat16
F32 = jnp.float32
STRIPS = (2, 3, 2, 1)


def after(value, *earlier):
    return lax.optimization_barrier((value,) + earlier)[0]


def z_route(step, sections, tensors):
    low_count = 4
    rows = sections // low_count
    cores = 2
    high_count = tensors // cores
    depth = low_count * high_count
    route = []
    for z in range(depth):
        origin = (z + step) % depth
        for y in range(rows):
            for core in range(cores):
                source = ((origin % low_count) * rows + y) * tensors + (origin // low_count) * cores + core
                target = ((z % low_count) * rows + y) * tensors + (z // low_count) * cores + core
                route.append((source, target))
    return route


def from_z(block, step):
    route = z_route(step, lax.axis_size("section"), lax.axis_size("tensor"))
    return lax.ppermute(block, ("section", "tensor"), route)


def from_x(block, step):
    count = lax.axis_size("ctx")
    return lax.ppermute(block, "ctx", [((c + step) % count, c) for c in range(count)])


def from_before(block, step):
    count = lax.axis_size("ctx")
    return lax.ppermute(block, "ctx", [(c - step, c) for c in range(step, count)])


def from_tensor(block, flip):
    count = lax.axis_size("tensor")
    return lax.ppermute(block, "tensor", [(t, t ^ flip) for t in range(count)])


def first_hop(shard):
    return from_x(shard, 1), from_x(shard, -1)


def second_hop(ahead, behind):
    half = ahead.shape[0] // 2
    return from_x(ahead[:half], 1), from_x(behind[half:], -1)


def rope_tables(rows):
    half = HEAD // 2
    exponent = jnp.arange(half).astype(F32) * (2.0 / HEAD)
    inverse = jnp.exp(-exponent * math.log(rope_base))
    positions = lax.axis_index("ctx") * rows + jnp.arange(rows, dtype=jnp.int32)
    angles = positions.astype(F32)[:, None] * inverse[None, :]
    cosine = jnp.cos(angles)
    sine = jnp.sin(angles)
    return jnp.concatenate((cosine, cosine), axis=1), jnp.concatenate((-sine, sine), axis=1)


def project_kernel(index_ref, normed_ref, own_ref, ahead_ref, across_ref, behind_ref, cosine_ref, sine_ref, out_ref, *, turned):
    shards = (own_ref, ahead_ref, across_ref, behind_ref)
    total = sum(
        jnp.dot(normed_ref[index_ref[step]], shard[...], preferred_element_type=F32)
        for step, shard in enumerate(shards)
    )
    for head in range(total.shape[1] // HEAD):
        raw = total[:, head * HEAD : (head + 1) * HEAD]
        if head < turned:
            raw = raw * cosine_ref[...] + pltpu.roll(raw, HEAD // 2, 1) * sine_ref[...]
        out_ref[:, head * HEAD : (head + 1) * HEAD] = raw.astype(BF)


def project(order, normed, shards, cosine, sine, turned, name):
    blocks, tokens, depth = normed.shape
    columns = shards[0].shape[1]
    wide = 2 * HEAD
    whole = lambda n, order: (0, 0)
    strip = lambda n, order: (0, n)
    return pl.pallas_call(
        functools.partial(project_kernel, turned=turned),
        grid_spec=pltpu.PrefetchScalarGridSpec(
            num_scalar_prefetch=1,
            grid=(columns // wide,),
            in_specs=[pl.BlockSpec((blocks, tokens, depth), lambda n, order: (0, 0, 0))]
            + [pl.BlockSpec((depth, wide), strip)] * 4
            + [pl.BlockSpec((tokens, HEAD), whole)] * 2,
            out_specs=pl.BlockSpec((tokens, wide), strip),
        ),
        out_shape=jax.ShapeDtypeStruct((tokens, columns), BF),
        compiler_params=pltpu.CompilerParams(vmem_limit_bytes=32 << 20),
        cost_estimate=pl.CostEstimate(flops=1024, transcendentals=0, bytes_accessed=1024),
        name=name,
    )(order, normed, *shards, cosine, sine)


def attend_kernel(query_ref, key_ref, value_ref, query_doc_ref, key_doc_ref, out_ref, bias_ref):
    rows, span = bias_ref.shape
    back = span - rows

    @pl.when(pl.program_id(1) == 0)
    def _():
        at_query = lax.broadcasted_iota(jnp.int32, (rows, span), 0)
        at_key = lax.broadcasted_iota(jnp.int32, (rows, span), 1) - back
        allowed = (at_key <= at_query) & (query_doc_ref[0] == key_doc_ref[0])
        bias_ref[...] = jnp.where(allowed, 0.0, -jnp.inf)

    for head in range(query_ref.shape[1] // HEAD):
        part = slice(head * HEAD, (head + 1) * HEAD)
        scores = lax.dot_general(
            query_ref[:, part], key_ref[0], (((1,), (1,)), ((), ())), preferred_element_type=F32
        )
        masked = scores + bias_ref[...]
        peak = jnp.max(masked, axis=1, keepdims=True)
        weights = jnp.exp((masked - peak) * (1.0 / math.sqrt(HEAD)))
        totals = jnp.sum(weights, axis=1, keepdims=True)
        mixed = jnp.dot(weights.astype(BF), value_ref[0], preferred_element_type=F32)
        out_ref[:, part] = (mixed / totals).astype(BF)


def attend(queries, pairs, query_docs, key_docs):
    batches, span, _ = pairs.shape
    rows = queries.shape[0] // batches
    wide = 2 * HEAD
    return pl.pallas_call(
        attend_kernel,
        grid=(batches, queries.shape[1] // wide),
        in_specs=[
            pl.BlockSpec((rows, wide), lambda b, h: (b, h)),
            pl.BlockSpec((1, span, HEAD), lambda b, h: (b, 0, 0)),
            pl.BlockSpec((1, span, HEAD), lambda b, h: (b, 0, 1)),
            pl.BlockSpec((1, rows, 1), lambda b, h: (b, 0, 0)),
            pl.BlockSpec((1, 1, span), lambda b, h: (b, 0, 0)),
        ],
        out_specs=pl.BlockSpec((rows, wide), lambda b, h: (b, h)),
        out_shape=jax.ShapeDtypeStruct(queries.shape, BF),
        scratch_shapes=[pltpu.VMEM((rows, span), F32)],
        compiler_params=pltpu.CompilerParams(vmem_limit_bytes=24 << 20),
        cost_estimate=pl.CostEstimate(flops=1024, transcendentals=0, bytes_accessed=1024),
        name="attend",
    )(queries, pairs, pairs, query_docs, key_docs)


def spread_kernel(index_ref, mixed_ref, own_ref, ahead_ref, across_ref, behind_ref, sent_ref, kept_ref, passed_ref, terms_ref):
    tokens = mixed_ref.shape[0]
    for step, shard in enumerate((own_ref, ahead_ref, across_ref, behind_ref)):
        terms_ref[step] = jnp.dot(mixed_ref[...], shard[...], preferred_element_type=F32)
    sent_ref[:tokens] = terms_ref[index_ref[1]].astype(BF)
    sent_ref[tokens:] = terms_ref[index_ref[3]].astype(BF)
    kept_ref[...] = terms_ref[index_ref[0]]
    passed_ref[...] = terms_ref[index_ref[2]]


def spread(order, mixed, shards, name):
    tokens, _ = mixed.shape
    columns = shards[0].shape[1]
    return pl.pallas_call(
        spread_kernel,
        in_specs=[pl.BlockSpec(memory_space=pltpu.SMEM)] + [pl.BlockSpec(memory_space=pltpu.VMEM)] * 5,
        out_specs=[pl.BlockSpec(memory_space=pltpu.VMEM)] * 3,
        out_shape=[
            jax.ShapeDtypeStruct((2 * tokens, columns), BF),
            jax.ShapeDtypeStruct((tokens, columns), F32),
            jax.ShapeDtypeStruct((tokens, columns), F32),
        ],
        scratch_shapes=[pltpu.VMEM((4, tokens, columns), F32)],
        compiler_params=pltpu.CompilerParams(vmem_limit_bytes=24 << 20),
        cost_estimate=pl.CostEstimate(flops=1024, transcendentals=0, bytes_accessed=1024),
        name=name,
    )(order, mixed, *shards)


def body(
    arriving,
    stored,
    docs_forward,
    docs_backward,
    norm_gain,
    query_weight,
    key_weight,
    value_projection_weight,
    out_weight,
):
    mine = arriving[0]
    held = stored[0]
    rows, width = mine.shape
    ring = lax.axis_size("ctx")
    c = lax.axis_index("ctx")
    t = lax.axis_index("tensor")
    near_high = lax.axis_index("section") < lax.axis_size("section") // 2
    docs = jnp.stack((docs_forward[0], docs_backward[0]), axis=0)
    flips = jnp.arange(4, dtype=jnp.int32)
    half = rows // 2

    strips = []
    start = 0
    for share in STRIPS:
        strips.append((start, start + width * share // sum(STRIPS)))
        start = strips[-1][1]
    out_own = [out_weight[0][:, low:high] for low, high in strips]

    q_weight = query_weight[0]
    with jax.named_scope("q_hop1"):
        q_ahead, q_behind = first_hop(q_weight)
    both = jnp.concatenate((mine, held), axis=0)
    with jax.named_scope("z_in"):
        up, down = from_z(both, 2), from_z(both, -2)
    kv_weight = jnp.concatenate((key_weight[0], value_projection_weight[0]), axis=1)
    with jax.named_scope("kv_hop1"):
        kv_ahead, kv_behind = first_hop(kv_weight)
    with jax.named_scope("far"):
        far_up, far_down = from_z(up[:half], 2), from_z(down[half:rows], -2)
    q_ahead, q_behind, kv_ahead, kv_behind, far_up, far_down, out_first = lax.optimization_barrier(
        (q_ahead, q_behind, kv_ahead, kv_behind, far_up, far_down, out_own[0])
    )

    with jax.named_scope("q_hop2"):
        q_across = jnp.concatenate(second_hop(q_ahead, q_behind), axis=0)
    with jax.named_scope("kv_hop2"):
        kv_across = jnp.concatenate(second_hop(kv_ahead, kv_behind), axis=0)
    with jax.named_scope("out_hop1_0"):
        out_hops = [first_hop(out_first)]
    mine_far = jnp.concatenate((far_up, far_down), axis=0)
    stashed = jnp.where(near_high, up[:rows], down[:rows])
    fetched = jnp.where(near_high, up[rows:], down[rows:])
    fetched_far = jnp.where(near_high, down[rows:], up[rows:])
    own_blocks = jnp.stack(
        (jnp.concatenate((mine, fetched), axis=0), jnp.concatenate((mine_far, fetched_far), axis=0)), axis=0
    )
    with jax.named_scope("sib"):
        sib_blocks = from_tensor(own_blocks, 1)

    gains = norm_gain[0].reshape(-1, width)
    stacked_flips = (0, 2, 1, 3)
    gain_blocks = jnp.stack(
        [lax.dynamic_index_in_dim(gains, t ^ j, 0, keepdims=True) for j in stacked_flips], axis=0
    ).astype(F32)

    def squares(blocks):
        return jnp.sum(jnp.square(blocks.astype(F32)), axis=(0, 2))[None, :, None]

    mean_square = (squares(own_blocks) + squares(sib_blocks)) * (1.0 / (width * ring))
    scale = lax.rsqrt(mean_square + norm_epsilon)
    normed = jnp.concatenate(
        (
            (own_blocks.astype(F32) * scale * gain_blocks[:2]).astype(BF),
            (sib_blocks.astype(F32) * scale * gain_blocks[2:]).astype(BF),
        ),
        axis=0,
    )
    cosine, sine = rope_tables(rows)
    cosine, sine = jnp.concatenate((cosine, cosine), axis=0), jnp.concatenate((sine, sine), axis=0)
    flip = t ^ ((c + flips) % ring)
    feature_order = (flip >> 1) + (flip & 1) * 2

    own_kv = project(
        feature_order,
        normed,
        (kv_weight, kv_ahead, kv_across, kv_behind),
        cosine,
        sine,
        1,
        "project_kv",
    )
    id_rows = 16
    ids = jnp.broadcast_to(docs.astype(BF)[:, None, :], (2, id_rows, rows))
    own_pair = jnp.concatenate((ids, own_kv.reshape(2, rows, 2 * HEAD)), axis=1)
    own_pair = after(own_pair, q_across, *out_hops[0])
    with jax.named_scope("kv_rows"):
        kv_one, kv_two = from_before(own_pair, 1), from_before(own_pair, 2)
    all_kv = jnp.concatenate((kv_two[:, id_rows:], kv_one[:, id_rows:], own_pair[:, id_rows:]), axis=1)
    docs_one = jnp.where(c >= 1, kv_one[:, 0].astype(jnp.int32), -1)
    docs_two = jnp.where(c >= 2, kv_two[:, 0].astype(jnp.int32), -1)
    key_docs = jnp.concatenate((docs_two, docs_one, docs), axis=1)
    queries = project(
        feature_order,
        after(normed, own_kv),
        (q_weight, q_ahead, q_across, q_behind),
        cosine,
        sine,
        2,
        "project_q",
    )
    with jax.named_scope("out_hop1_1"):
        out_hops.append(first_hop(after(out_own[1], *out_hops[0])))
    mixed = attend(queries, all_kv, docs[:, :, None], key_docs[:, None, :])

    residual = jnp.concatenate((mine, fetched), axis=0)
    term_order = ((t ^ flips) - c) % ring
    passed_before = []
    outputs = []
    for index, (low, high) in enumerate(strips):
        ahead, behind = out_hops[index]
        with jax.named_scope("out_hop2_%d" % index):
            across = from_x(ahead, 1) if index % 2 == 0 else from_x(behind, -1)
        following = out_hops[index + 1] if index + 1 < len(strips) else ()
        if index + 2 < len(strips):
            with jax.named_scope("out_hop1_%d" % (index + 2)):
                out_hops.append(first_hop(after(out_own[index + 2], *following)))
        sent, kept, passed = spread(
            term_order,
            after(mixed, *(following if index else ()), *passed_before, *(outputs[-1:] if index + 1 < len(strips) else outputs[-2:-1])),
            (out_own[index], ahead, across, behind),
            "spread_%d" % index,
        )
        if index + 1 == len(strips):
            sent = after(sent, outputs[-1])
        with jax.named_scope("core_sum_%d" % index):
            received = from_tensor(sent, 1)
        kept = kept + received[: 2 * rows].astype(F32)
        passed = (passed + received[2 * rows :].astype(F32)).astype(BF)
        with jax.named_scope("z_sum_%d" % index):
            arrived = from_tensor(passed, 2)
        passed_before = [passed]
        base = residual[:, low:high].astype(F32)
        outputs.append((base + (kept + arrived.astype(F32))).astype(BF))
    result = jnp.concatenate(outputs, axis=1)
    return (result[:rows][None], stashed[None], result[rows:][None])


def solution(mesh):
    return jax.shard_map(
        body,
        mesh=mesh,
        in_specs=(
            P("section", "ctx", "tensor"),
            P("section", "ctx", "tensor"),
            P("section", "ctx"),
            P("section", "ctx"),
            P("section", None),
            P("section", "ctx", "tensor"),
            P("section", "ctx", "tensor"),
            P("section", "ctx", "tensor"),
            P("section", "tensor", "ctx"),
        ),
        out_specs=(
            P("section", "ctx", "tensor"),
            P("section", "ctx", "tensor"),
            P("section", "ctx", "tensor"),
        ),
        check_vma=False,
    )
```

```python
import functools
import math

import jax
import jax.numpy as jnp
from jax import lax
from jax.experimental import pallas as pl
from jax.experimental.pallas import tpu as pltpu
from jax.sharding import PartitionSpec as P

HEAD = 128
norm_epsilon = 1e-05
rope_base = 500000.0
BF = jnp.bfloat16
F32 = jnp.float32
STRIPS = (5, 3)


def after(value, *earlier):
    return lax.optimization_barrier((value,) + earlier)[0]


def z_route(step, sections, tensors):
    low_count = 4
    rows = sections // low_count
    cores = 2
    high_count = tensors // cores
    depth = low_count * high_count
    route = []
    for z in range(depth):
        origin = (z + step) % depth
        for y in range(rows):
            for core in range(cores):
                source = ((origin % low_count) * rows + y) * tensors + (origin // low_count) * cores + core
                target = ((z % low_count) * rows + y) * tensors + (z // low_count) * cores + core
                route.append((source, target))
    return route


def from_z(block, step):
    route = z_route(step, lax.axis_size("section"), lax.axis_size("tensor"))
    return lax.ppermute(block, ("section", "tensor"), route)


def from_x(block, step):
    count = lax.axis_size("ctx")
    return lax.ppermute(block, "ctx", [((c + step) % count, c) for c in range(count)])


def from_before(block, step):
    count = lax.axis_size("ctx")
    return lax.ppermute(block, "ctx", [(c - step, c) for c in range(step, count)])


def from_tensor(block, flip):
    count = lax.axis_size("tensor")
    return lax.ppermute(block, "tensor", [(t, t ^ flip) for t in range(count)])


def first_hop(shard):
    return from_x(shard, 1), from_x(shard, -1)


def second_hop(ahead, behind):
    half = ahead.shape[0] // 2
    return from_x(ahead[:half], 1), from_x(behind[half:], -1)


def rope_tables(rows):
    half = HEAD // 2
    exponent = jnp.arange(half).astype(F32) * (2.0 / HEAD)
    inverse = jnp.exp(-exponent * math.log(rope_base))
    positions = lax.axis_index("ctx") * rows + jnp.arange(rows, dtype=jnp.int32)
    angles = positions.astype(F32)[:, None] * inverse[None, :]
    cosine = jnp.cos(angles)
    sine = jnp.sin(angles)
    return jnp.concatenate((cosine, cosine), axis=1), jnp.concatenate((-sine, sine), axis=1)


def normalize_kernel(*refs):
    block_refs, gain_ref, out_ref = refs[:8], refs[8], refs[9]
    for batch in range(2):
        blocks = [ref[...].astype(F32) for ref in block_refs[4 * batch : 4 * batch + 4]]
        total = sum(jnp.sum(block * block, axis=1, keepdims=True) for block in blocks)
        scale = lax.rsqrt(total * (1.0 / (blocks[0].shape[1] * len(blocks))) + norm_epsilon)
        for flip, block in enumerate(blocks):
            gain = gain_ref[flip : flip + 1].astype(F32)
            out_ref[flip, batch] = (block * scale * gain).astype(BF)


def normalize(blocks, gains, rows):
    width = gains.shape[1]
    step = 64
    split = [
        pl.BlockSpec((step, width), functools.partial(lambda skip, n: (skip + n, 0), part * (rows // step)))
        for _, part in blocks
    ]
    out = pl.pallas_call(
        normalize_kernel,
        grid=(rows // step,),
        in_specs=split + [pl.BlockSpec(gains.shape, lambda n: (0, 0))],
        out_specs=pl.BlockSpec((4, 2, step, width), lambda n: (0, 0, n, 0)),
        out_shape=jax.ShapeDtypeStruct((4, 2, rows, width), BF),
        compiler_params=pltpu.CompilerParams(vmem_limit_bytes=24 << 20),
        cost_estimate=pl.CostEstimate(flops=1024, transcendentals=0, bytes_accessed=1024),
        name="normalize",
    )(*[array for array, _ in blocks], gains)
    return out.reshape(4, 2 * rows, width)


def project_kernel(index_ref, normed_ref, own_ref, ahead_ref, across_ref, behind_ref, cosine_ref, sine_ref, out_ref, *, turned):
    shards = (own_ref, ahead_ref, across_ref, behind_ref)
    total = sum(
        jnp.dot(normed_ref[index_ref[step]], shard[...], preferred_element_type=F32)
        for step, shard in enumerate(shards)
    )
    for head in range(total.shape[1] // HEAD):
        raw = total[:, head * HEAD : (head + 1) * HEAD]
        if head < turned:
            raw = raw * cosine_ref[...] + pltpu.roll(raw, HEAD // 2, 1) * sine_ref[...]
        out_ref[:, head * HEAD : (head + 1) * HEAD] = raw.astype(BF)


def project(order, normed, shards, cosine, sine, turned, name):
    blocks, tokens, depth = normed.shape
    columns = shards[0].shape[1]
    wide = 2 * HEAD
    whole = lambda n, order: (0, 0)
    strip = lambda n, order: (0, n)
    return pl.pallas_call(
        functools.partial(project_kernel, turned=turned),
        grid_spec=pltpu.PrefetchScalarGridSpec(
            num_scalar_prefetch=1,
            grid=(columns // wide,),
            in_specs=[pl.BlockSpec((blocks, tokens, depth), lambda n, order: (0, 0, 0))]
            + [pl.BlockSpec((depth, wide), strip)] * 4
            + [pl.BlockSpec((tokens, HEAD), whole)] * 2,
            out_specs=pl.BlockSpec((tokens, wide), strip),
        ),
        out_shape=jax.ShapeDtypeStruct((tokens, columns), BF),
        compiler_params=pltpu.CompilerParams(vmem_limit_bytes=32 << 20),
        cost_estimate=pl.CostEstimate(flops=1024, transcendentals=0, bytes_accessed=1024),
        name=name,
    )(order, normed, *shards, cosine, sine)


def attend_kernel(query_ref, key_ref, value_ref, query_doc_ref, key_doc_ref, out_ref, bias_ref):
    rows, span = bias_ref.shape
    back = span - rows

    @pl.when(pl.program_id(1) == 0)
    def _():
        at_query = lax.broadcasted_iota(jnp.int32, (rows, span), 0)
        at_key = lax.broadcasted_iota(jnp.int32, (rows, span), 1) - back
        allowed = (at_key <= at_query) & (query_doc_ref[0] == key_doc_ref[0])
        bias_ref[...] = jnp.where(allowed, 0.0, -jnp.inf)

    for head in range(query_ref.shape[1] // HEAD):
        part = slice(head * HEAD, (head + 1) * HEAD)
        scores = lax.dot_general(
            query_ref[:, part], key_ref[0], (((1,), (1,)), ((), ())), preferred_element_type=F32
        )
        masked = scores + bias_ref[...]
        peak = jnp.max(masked, axis=1, keepdims=True)
        weights = jnp.exp((masked - peak) * (1.0 / math.sqrt(HEAD)))
        totals = jnp.sum(weights, axis=1, keepdims=True)
        mixed = jnp.dot(weights.astype(BF), value_ref[0], preferred_element_type=F32)
        out_ref[:, part] = (mixed / totals).astype(BF)


def attend(queries, pairs, query_docs, key_docs):
    batches, span, _ = pairs.shape
    rows = queries.shape[0] // batches
    wide = 2 * HEAD
    return pl.pallas_call(
        attend_kernel,
        grid=(batches, queries.shape[1] // wide),
        in_specs=[
            pl.BlockSpec((rows, wide), lambda b, h: (b, h)),
            pl.BlockSpec((1, span, HEAD), lambda b, h: (b, 0, 0)),
            pl.BlockSpec((1, span, HEAD), lambda b, h: (b, 0, 1)),
            pl.BlockSpec((1, rows, 1), lambda b, h: (b, 0, 0)),
            pl.BlockSpec((1, 1, span), lambda b, h: (b, 0, 0)),
        ],
        out_specs=pl.BlockSpec((rows, wide), lambda b, h: (b, h)),
        out_shape=jax.ShapeDtypeStruct(queries.shape, BF),
        scratch_shapes=[pltpu.VMEM((rows, span), F32)],
        compiler_params=pltpu.CompilerParams(vmem_limit_bytes=24 << 20),
        cost_estimate=pl.CostEstimate(flops=1024, transcendentals=0, bytes_accessed=1024),
        name="attend",
    )(queries, pairs, pairs, query_docs, key_docs)


def spread_kernel(index_ref, mixed_ref, own_ref, ahead_ref, across_ref, behind_ref, sent_kept_ref, sent_passed_ref, kept_ref, passed_ref, terms_ref):
    for step, shard in enumerate((own_ref, ahead_ref, across_ref, behind_ref)):
        terms_ref[step] = jnp.dot(mixed_ref[...], shard[...], preferred_element_type=F32)
    sent_kept_ref[...] = terms_ref[index_ref[1]].astype(BF)
    sent_passed_ref[...] = terms_ref[index_ref[3]].astype(BF)
    kept_ref[...] = terms_ref[index_ref[0]]
    passed_ref[...] = terms_ref[index_ref[2]]


def spread(order, mixed, shards, name):
    tokens, _ = mixed.shape
    columns = shards[0].shape[1]
    return pl.pallas_call(
        spread_kernel,
        in_specs=[pl.BlockSpec(memory_space=pltpu.SMEM)] + [pl.BlockSpec(memory_space=pltpu.VMEM)] * 5,
        out_specs=[pl.BlockSpec(memory_space=pltpu.VMEM)] * 4,
        out_shape=[
            jax.ShapeDtypeStruct((tokens, columns), BF),
            jax.ShapeDtypeStruct((tokens, columns), BF),
            jax.ShapeDtypeStruct((tokens, columns), F32),
            jax.ShapeDtypeStruct((tokens, columns), F32),
        ],
        scratch_shapes=[pltpu.VMEM((4, tokens, columns), F32)],
        compiler_params=pltpu.CompilerParams(vmem_limit_bytes=24 << 20),
        cost_estimate=pl.CostEstimate(flops=1024, transcendentals=0, bytes_accessed=1024),
        name=name,
    )(order, mixed, *shards)


def body(
    arriving,
    stored,
    docs_forward,
    docs_backward,
    norm_gain,
    query_weight,
    key_weight,
    value_projection_weight,
    out_weight,
):
    mine = arriving[0]
    held = stored[0]
    rows, width = mine.shape
    ring = lax.axis_size("ctx")
    c = lax.axis_index("ctx")
    t = lax.axis_index("tensor")
    near_high = lax.axis_index("section") < lax.axis_size("section") // 2
    docs = jnp.stack((docs_forward[0], docs_backward[0]), axis=0)
    flips = jnp.arange(4, dtype=jnp.int32)
    half = rows // 2

    strips = []
    start = 0
    for share in STRIPS:
        strips.append((start, start + width * share // sum(STRIPS)))
        start = strips[-1][1]
    out_own = [out_weight[0][:, low:high] for low, high in strips]

    kv_weight = jnp.concatenate((key_weight[0], value_projection_weight[0]), axis=1)
    with jax.named_scope("kv_hop1"):
        kv_ahead, kv_behind = first_hop(kv_weight)
    both = jnp.concatenate((mine, held), axis=0)
    with jax.named_scope("z_in"):
        up, down = from_z(both, 2), from_z(both, -2)
    q_weight = query_weight[0]
    with jax.named_scope("q_hop1"):
        q_ahead, q_behind = first_hop(after(q_weight, kv_ahead, kv_behind))
    stashed = jnp.where(near_high, up[:rows], down[:rows])
    fetched = jnp.where(near_high, up[rows:], down[rows:])
    fetched_far = jnp.where(near_high, down[rows:], up[rows:])
    near_blocks = jnp.concatenate((mine, fetched, fetched_far), axis=0)
    with jax.named_scope("sib_near"):
        sib_near = from_tensor(near_blocks, 1)
    up, down, q_ahead, q_behind, kv_ahead, kv_behind, sib_near = lax.optimization_barrier(
        (up, down, q_ahead, q_behind, kv_ahead, kv_behind, sib_near)
    )

    with jax.named_scope("kv_hop2"):
        kv_across = jnp.concatenate(second_hop(kv_ahead, kv_behind), axis=0)
    with jax.named_scope("q_hop2"):
        q_across = jnp.concatenate(second_hop(q_ahead, q_behind), axis=0)
    with jax.named_scope("far"):
        mine_far = jnp.concatenate((from_z(up[:half], 2), from_z(down[half:rows], -2)), axis=0)
    with jax.named_scope("out_hop1_0"):
        out_hops = [first_hop(after(out_own[0], kv_across))]
    with jax.named_scope("sib_far"):
        sib_far = from_tensor(mine_far, 1)
    blocks = (
        ((mine, 0), (sib_near, 0), (mine_far, 0), (sib_far, 0))
        + ((fetched, 0), (sib_near, 1), (fetched_far, 0), (sib_near, 2))
    )
    gains = norm_gain[0].reshape(-1, width)
    normed = normalize(blocks, jnp.take(gains, t ^ flips, axis=0), rows)
    cosine, sine = rope_tables(rows)
    cosine, sine = jnp.concatenate((cosine, cosine), axis=0), jnp.concatenate((sine, sine), axis=0)
    feature_order = t ^ ((c + flips) % ring)

    own_kv = project(
        feature_order,
        after(normed, q_across),
        (kv_weight, kv_ahead, kv_across, kv_behind),
        cosine,
        sine,
        1,
        "project_kv",
    )
    id_rows = 16
    ids = jnp.broadcast_to(docs.astype(BF)[:, None, :], (2, id_rows, rows))
    own_pair = jnp.concatenate((ids, own_kv.reshape(2, rows, 2 * HEAD)), axis=1)
    with jax.named_scope("kv_rows"):
        kv_one, kv_two = from_before(own_pair, 1), from_before(own_pair, 2)
    all_kv = jnp.concatenate((kv_two[:, id_rows:], kv_one[:, id_rows:], own_pair[:, id_rows:]), axis=1)
    docs_one = jnp.where(c >= 1, kv_one[:, 0].astype(jnp.int32), -1)
    docs_two = jnp.where(c >= 2, kv_two[:, 0].astype(jnp.int32), -1)
    key_docs = jnp.concatenate((docs_two, docs_one, docs), axis=1)
    queries = project(
        feature_order,
        after(normed, own_kv),
        (q_weight, q_ahead, q_across, q_behind),
        cosine,
        sine,
        2,
        "project_q",
    )
    mixed = attend(queries, all_kv, docs[:, :, None], key_docs[:, None, :])

    residual = jnp.concatenate((mine, fetched), axis=0)
    term_order = ((t ^ flips) - c) % ring
    passed_before = []
    outputs = []
    for index, (low, high) in enumerate(strips):
        ahead, behind = out_hops[index]
        with jax.named_scope("out_hop2_%d" % index):
            across = jnp.concatenate(second_hop(ahead, behind), axis=0)
        if index + 1 < len(strips):
            with jax.named_scope("out_hop1_%d" % (index + 1)):
                out_hops.append(first_hop(after(out_own[index + 1], across)))
        sent_kept, sent_passed, kept, passed = spread(
            term_order, after(mixed, *passed_before), (out_own[index], ahead, across, behind), "spread_%d" % index
        )
        if index:
            sent_passed = after(sent_passed, outputs[-1])
        with jax.named_scope("core_passed_%d" % index):
            passed = (passed + from_tensor(sent_passed, 1).astype(F32)).astype(BF)
        with jax.named_scope("z_sum_%d" % index):
            arrived = from_tensor(passed, 2)
        with jax.named_scope("core_kept_%d" % index):
            kept = kept + from_tensor(sent_kept, 1).astype(F32)
        passed_before = [passed]
        base = residual[:, low:high].astype(F32)
        outputs.append((base + (kept + arrived.astype(F32))).astype(BF))
    result = jnp.concatenate(outputs, axis=1)
    return (result[:rows][None], stashed[None], result[rows:][None])


def solution(mesh):
    return jax.shard_map(
        body,
        mesh=mesh,
        in_specs=(
            P("section", "ctx", "tensor"),
            P("section", "ctx", "tensor"),
            P("section", "ctx"),
            P("section", "ctx"),
            P("section", None),
            P("section", "ctx", "tensor"),
            P("section", "ctx", "tensor"),
            P("section", "ctx", "tensor"),
            P("section", "tensor", "ctx"),
        ),
        out_specs=(
            P("section", "ctx", "tensor"),
            P("section", "ctx", "tensor"),
            P("section", "ctx", "tensor"),
        ),
        check_vma=False,
    )
```

```python
import functools
import math

import jax
import jax.numpy as jnp
from jax import lax
from jax.experimental import pallas as pl
from jax.experimental.pallas import tpu as pltpu
from jax.sharding import PartitionSpec as P

HEAD = 128
norm_epsilon = 1e-05
rope_base = 500000.0
BF = jnp.bfloat16
F32 = jnp.float32
STRIPS = (1, 1)
HOLD_FLOPS = 10**10


def after(value, *earlier):
    return lax.optimization_barrier((value,) + earlier)[0]


def hold_kernel(*refs):
    del refs


def hold(value, *earlier):
    anywhere = pl.BlockSpec(memory_space=pl.ANY)
    return pl.pallas_call(
        hold_kernel,
        in_specs=[anywhere] * (1 + len(earlier)),
        out_specs=anywhere,
        out_shape=jax.ShapeDtypeStruct(value.shape, value.dtype),
        input_output_aliases={0: 0},
        cost_estimate=pl.CostEstimate(flops=HOLD_FLOPS, transcendentals=0, bytes_accessed=1024),
        name="hold",
    )(value, *earlier)


def z_route(step, sections, tensors):
    low_count = 4
    rows = sections // low_count
    cores = 2
    high_count = tensors // cores
    depth = low_count * high_count
    route = []
    for z in range(depth):
        origin = (z + step) % depth
        for y in range(rows):
            for core in range(cores):
                source = ((origin % low_count) * rows + y) * tensors + (origin // low_count) * cores + core
                target = ((z % low_count) * rows + y) * tensors + (z // low_count) * cores + core
                route.append((source, target))
    return route


def from_z(block, step):
    route = z_route(step, lax.axis_size("section"), lax.axis_size("tensor"))
    return lax.ppermute(block, ("section", "tensor"), route)


def from_x(block, step):
    count = lax.axis_size("ctx")
    return lax.ppermute(block, "ctx", [((c + step) % count, c) for c in range(count)])


def from_before(block, step):
    count = lax.axis_size("ctx")
    return lax.ppermute(block, "ctx", [(c - step, c) for c in range(step, count)])


def from_tensor(block, flip):
    count = lax.axis_size("tensor")
    return lax.ppermute(block, "tensor", [(t, t ^ flip) for t in range(count)])


def first_hop(shard):
    return from_x(shard, 1), from_x(shard, -1)


def second_hop(ahead, behind):
    half = ahead.shape[0] // 2
    return from_x(ahead[:half], 1), from_x(behind[half:], -1)


def rope_tables(rows):
    half = HEAD // 2
    exponent = jnp.arange(half).astype(F32) * (2.0 / HEAD)
    inverse = jnp.exp(-exponent * math.log(rope_base))
    positions = lax.axis_index("ctx") * rows + jnp.arange(rows, dtype=jnp.int32)
    angles = positions.astype(F32)[:, None] * inverse[None, :]
    cosine = jnp.cos(angles)
    sine = jnp.sin(angles)
    return jnp.concatenate((cosine, cosine), axis=1), jnp.concatenate((-sine, sine), axis=1)


def normalize_kernel(*refs):
    block_refs, gain_ref, out_ref = refs[:8], refs[8], refs[9]
    for batch in range(2):
        blocks = [ref[...].astype(F32) for ref in block_refs[4 * batch : 4 * batch + 4]]
        total = sum(jnp.sum(block * block, axis=1, keepdims=True) for block in blocks)
        scale = lax.rsqrt(total * (1.0 / (blocks[0].shape[1] * len(blocks))) + norm_epsilon)
        for flip, block in enumerate(blocks):
            gain = gain_ref[flip : flip + 1].astype(F32)
            out_ref[flip, batch] = (block * scale * gain).astype(BF)


def normalize(blocks, gains, rows):
    width = gains.shape[1]
    step = 64
    split = [
        pl.BlockSpec((step, width), functools.partial(lambda skip, n: (skip + n, 0), part * (rows // step)))
        for _, part in blocks
    ]
    out = pl.pallas_call(
        normalize_kernel,
        grid=(rows // step,),
        in_specs=split + [pl.BlockSpec(gains.shape, lambda n: (0, 0))],
        out_specs=pl.BlockSpec((4, 2, step, width), lambda n: (0, 0, n, 0)),
        out_shape=jax.ShapeDtypeStruct((4, 2, rows, width), BF),
        compiler_params=pltpu.CompilerParams(vmem_limit_bytes=24 << 20),
        cost_estimate=pl.CostEstimate(flops=1024, transcendentals=0, bytes_accessed=1024),
        name="normalize",
    )(*[array for array, _ in blocks], gains)
    return out.reshape(4, 2 * rows, width)


def project_kernel(index_ref, normed_ref, *refs, pieces, turned):
    piece_refs, (cosine_ref, sine_ref, out_ref) = refs[: len(pieces)], refs[len(pieces) :]
    total = sum(
        jnp.dot(
            normed_ref[index_ref[step], :, low : low + ref.shape[0]], ref[...], preferred_element_type=F32
        )
        for (step, low), ref in zip(pieces, piece_refs)
    )
    for head in range(total.shape[1] // HEAD):
        raw = total[:, head * HEAD : (head + 1) * HEAD]
        if head < turned:
            raw = raw * cosine_ref[...] + pltpu.roll(raw, HEAD // 2, 1) * sine_ref[...]
        out_ref[:, head * HEAD : (head + 1) * HEAD] = raw.astype(BF)


def project(order, normed, shards, cosine, sine, turned, name):
    blocks, tokens, depth = normed.shape
    arrays = [array for array, _, _ in shards]
    columns = arrays[0].shape[1]
    wide = 2 * HEAD
    whole = lambda n, order: (0, 0)
    strip = lambda n, order: (0, n)
    return pl.pallas_call(
        functools.partial(project_kernel, pieces=[(step, low) for _, step, low in shards], turned=turned),
        grid_spec=pltpu.PrefetchScalarGridSpec(
            num_scalar_prefetch=1,
            grid=(columns // wide,),
            in_specs=[pl.BlockSpec((blocks, tokens, depth), lambda n, order: (0, 0, 0))]
            + [pl.BlockSpec((array.shape[0], wide), strip) for array in arrays]
            + [pl.BlockSpec((tokens, HEAD), whole)] * 2,
            out_specs=pl.BlockSpec((tokens, wide), strip),
        ),
        out_shape=jax.ShapeDtypeStruct((tokens, columns), BF),
        compiler_params=pltpu.CompilerParams(vmem_limit_bytes=32 << 20),
        cost_estimate=pl.CostEstimate(flops=1024, transcendentals=0, bytes_accessed=1024),
        name=name,
    )(order, normed, *arrays, cosine, sine)


def attend_kernel(query_ref, key_ref, value_ref, query_doc_ref, key_doc_ref, out_ref, bias_ref):
    rows, span = bias_ref.shape
    back = span - rows

    @pl.when(pl.program_id(1) == 0)
    def _():
        at_query = lax.broadcasted_iota(jnp.int32, (rows, span), 0)
        at_key = lax.broadcasted_iota(jnp.int32, (rows, span), 1) - back
        allowed = (at_key <= at_query) & (query_doc_ref[0] == key_doc_ref[0])
        bias_ref[...] = jnp.where(allowed, 0.0, -jnp.inf)

    for head in range(query_ref.shape[1] // HEAD):
        part = slice(head * HEAD, (head + 1) * HEAD)
        scores = lax.dot_general(
            query_ref[:, part], key_ref[0], (((1,), (1,)), ((), ())), preferred_element_type=F32
        )
        masked = scores + bias_ref[...]
        peak = jnp.max(masked, axis=1, keepdims=True)
        weights = jnp.exp((masked - peak) * (1.0 / math.sqrt(HEAD)))
        totals = jnp.sum(weights, axis=1, keepdims=True)
        mixed = jnp.dot(weights.astype(BF), value_ref[0], preferred_element_type=F32)
        out_ref[:, part] = (mixed / totals).astype(BF)


def attend(queries, pairs, query_docs, key_docs):
    batches, span, _ = pairs.shape
    rows = queries.shape[0] // batches
    wide = 2 * HEAD
    return pl.pallas_call(
        attend_kernel,
        grid=(batches, queries.shape[1] // wide),
        in_specs=[
            pl.BlockSpec((rows, wide), lambda b, h: (b, h)),
            pl.BlockSpec((1, span, HEAD), lambda b, h: (b, 0, 0)),
            pl.BlockSpec((1, span, HEAD), lambda b, h: (b, 0, 1)),
            pl.BlockSpec((1, rows, 1), lambda b, h: (b, 0, 0)),
            pl.BlockSpec((1, 1, span), lambda b, h: (b, 0, 0)),
        ],
        out_specs=pl.BlockSpec((rows, wide), lambda b, h: (b, h)),
        out_shape=jax.ShapeDtypeStruct(queries.shape, BF),
        scratch_shapes=[pltpu.VMEM((rows, span), F32)],
        compiler_params=pltpu.CompilerParams(vmem_limit_bytes=24 << 20),
        cost_estimate=pl.CostEstimate(flops=1024, transcendentals=0, bytes_accessed=1024),
        name="attend",
    )(queries, pairs, pairs, query_docs, key_docs)


def spread_kernel(
    index_ref, mixed_ref, own_ref, ahead_ref, near_ref, back_ref, behind_ref,
    sent_kept_ref, sent_passed_ref, kept_ref, passed_ref, terms_ref,
):
    half = near_ref.shape[0]
    for step, shard in ((0, own_ref), (1, ahead_ref), (3, behind_ref)):
        terms_ref[step] = jnp.dot(mixed_ref[...], shard[...], preferred_element_type=F32)
    terms_ref[2] = jnp.dot(mixed_ref[:, :half], near_ref[...], preferred_element_type=F32) + jnp.dot(
        mixed_ref[:, half:], back_ref[...], preferred_element_type=F32
    )
    sent_kept_ref[...] = terms_ref[index_ref[1]].astype(BF)
    sent_passed_ref[...] = terms_ref[index_ref[3]].astype(BF)
    kept_ref[...] = terms_ref[index_ref[0]]
    passed_ref[...] = terms_ref[index_ref[2]]


def spread(order, mixed, shards, name):
    tokens, _ = mixed.shape
    columns = shards[0].shape[1]
    return pl.pallas_call(
        spread_kernel,
        in_specs=[pl.BlockSpec(memory_space=pltpu.SMEM)] + [pl.BlockSpec(memory_space=pltpu.VMEM)] * 6,
        out_specs=[pl.BlockSpec(memory_space=pltpu.VMEM)] * 4,
        out_shape=[
            jax.ShapeDtypeStruct((tokens, columns), BF),
            jax.ShapeDtypeStruct((tokens, columns), BF),
            jax.ShapeDtypeStruct((tokens, columns), F32),
            jax.ShapeDtypeStruct((tokens, columns), F32),
        ],
        scratch_shapes=[pltpu.VMEM((4, tokens, columns), F32)],
        compiler_params=pltpu.CompilerParams(vmem_limit_bytes=24 << 20),
        cost_estimate=pl.CostEstimate(flops=1024, transcendentals=0, bytes_accessed=1024),
        name=name,
    )(order, mixed, *shards)


def body(
    arriving,
    stored,
    docs_forward,
    docs_backward,
    norm_gain,
    query_weight,
    key_weight,
    value_projection_weight,
    out_weight,
):
    mine = arriving[0]
    held = stored[0]
    rows, width = mine.shape
    ring = lax.axis_size("ctx")
    c = lax.axis_index("ctx")
    t = lax.axis_index("tensor")
    near_high = lax.axis_index("section") < lax.axis_size("section") // 2
    docs = jnp.stack((docs_forward[0], docs_backward[0]), axis=0)
    flips = jnp.arange(4, dtype=jnp.int32)
    half = rows // 2

    strips = []
    start = 0
    for share in STRIPS:
        strips.append((start, start + width * share // sum(STRIPS)))
        start = strips[-1][1]
    out_own = [out_weight[0][:, low:high] for low, high in strips]

    kv_weight = jnp.concatenate((key_weight[0], value_projection_weight[0]), axis=1)
    with jax.named_scope("kv_hop1"):
        kv_ahead, kv_behind = first_hop(kv_weight)
    both = jnp.concatenate((mine, held), axis=0)
    with jax.named_scope("z_in"):
        up, down = from_z(both, 2), from_z(both, -2)
    with jax.named_scope("far"):
        mine_far = from_tensor(mine, 2)
    q_weight = query_weight[0]
    depth = q_weight.shape[0] // 2
    with jax.named_scope("q_hop1"):
        q_ahead, q_behind = first_hop(after(q_weight, kv_ahead, kv_behind))
    q_ahead, q_behind, kv_ahead, up, down, mine_far = lax.optimization_barrier(
        (q_ahead, q_behind, kv_ahead, up, down, mine_far)
    )
    with jax.named_scope("q_hop2"):
        across_low, across_high = second_hop(q_ahead, q_behind)
    with jax.named_scope("kv_hop2"):
        kv_across = from_x(kv_ahead, 1)

    stashed = jnp.where(near_high, up[:rows], down[:rows])
    fetched = jnp.where(near_high, up[rows:], down[rows:])
    fetched_far = jnp.where(near_high, down[rows:], up[rows:])
    with jax.named_scope("sib"):
        sib = from_tensor(jnp.concatenate((mine, fetched, fetched_far, mine_far), axis=0), 1)
    blocks = (
        ((mine, 0), (sib, 0), (mine_far, 0), (sib, 3))
        + ((fetched, 0), (sib, 1), (fetched_far, 0), (sib, 2))
    )
    gains = norm_gain[0].reshape(-1, width)
    normed = normalize(blocks, jnp.take(gains, t ^ flips, axis=0), rows)
    cosine, sine = rope_tables(rows)
    cosine, sine = jnp.concatenate((cosine, cosine), axis=0), jnp.concatenate((sine, sine), axis=0)
    feature_order = t ^ ((c + flips) % ring)

    own_kv = project(
        feature_order,
        normed,
        ((kv_weight, 0, 0), (kv_ahead, 1, 0), (kv_across, 2, 0), (kv_behind, 3, 0)),
        cosine,
        sine,
        1,
        "project_kv",
    )
    id_rows = 16
    ids = jnp.broadcast_to(docs.astype(BF)[:, None, :], (2, id_rows, rows))
    own_pair = jnp.concatenate((ids, own_kv.reshape(2, rows, 2 * HEAD)), axis=1)
    with jax.named_scope("kv_rows"):
        kv_one, kv_two = from_before(own_pair, 1), from_before(own_pair, 2)
    with jax.named_scope("out_hop1_0"):
        out_hops = [first_hop(hold(out_own[0], across_low, across_high, kv_across))]
    all_kv = jnp.concatenate((kv_two[:, id_rows:], kv_one[:, id_rows:], own_pair[:, id_rows:]), axis=1)
    docs_one = jnp.where(c >= 1, kv_one[:, 0].astype(jnp.int32), -1)
    docs_two = jnp.where(c >= 2, kv_two[:, 0].astype(jnp.int32), -1)
    key_docs = jnp.concatenate((docs_two, docs_one, docs), axis=1)
    queries = project(
        feature_order,
        after(normed, own_kv),
        (
            (q_weight, 0, 0),
            (q_ahead, 1, 0),
            (q_behind, 3, 0),
            (across_low, 2, 0),
            (across_high, 2, depth),
        ),
        cosine,
        sine,
        2,
        "project_q",
    )
    mixed = attend(queries, all_kv, docs[:, :, None], key_docs[:, None, :])

    residual = jnp.concatenate((mine, fetched), axis=0)
    term_order = ((t ^ flips) - c) % ring
    passed_before = []
    outputs = []
    for index, (low, high) in enumerate(strips):
        ahead, behind = out_hops[index]
        with jax.named_scope("out_hop2_%d" % index):
            near, back = second_hop(ahead, behind)
        if index + 1 < len(strips):
            with jax.named_scope("out_hop1_%d" % (index + 1)):
                out_hops.append(first_hop(after(out_own[index + 1], ahead, behind)))
        sent_kept, sent_passed, kept, passed = spread(
            term_order,
            after(mixed, *passed_before),
            (out_own[index], ahead, near, back, behind),
            "spread_%d" % index,
        )
        with jax.named_scope("core_passed_%d" % index):
            passed = (passed + from_tensor(sent_passed, 1).astype(F32)).astype(BF)
        if index:
            passed = after(passed, outputs[-1])
        with jax.named_scope("z_sum_%d" % index):
            arrived = from_tensor(passed, 2)
        with jax.named_scope("core_kept_%d" % index):
            kept = kept + from_tensor(sent_kept, 1).astype(F32)
        passed_before = [passed]
        base = residual[:, low:high].astype(F32)
        outputs.append((base + (kept + arrived.astype(F32))).astype(BF))
    result = jnp.concatenate(outputs, axis=1)
    return (result[:rows][None], stashed[None], result[rows:][None])


def solution(mesh):
    return jax.shard_map(
        body,
        mesh=mesh,
        in_specs=(
            P("section", "ctx", "tensor"),
            P("section", "ctx", "tensor"),
            P("section", "ctx"),
            P("section", "ctx"),
            P("section", None),
            P("section", "ctx", "tensor"),
            P("section", "ctx", "tensor"),
            P("section", "ctx", "tensor"),
            P("section", "tensor", "ctx"),
        ),
        out_specs=(
            P("section", "ctx", "tensor"),
            P("section", "ctx", "tensor"),
            P("section", "ctx", "tensor"),
        ),
        check_vma=False,
    )
```

```python
import functools
import math

import jax
import jax.numpy as jnp
from jax import lax
from jax.experimental import pallas as pl
from jax.experimental.pallas import tpu as pltpu
from jax.sharding import PartitionSpec as P

HEAD = 128
norm_epsilon = 1e-05
rope_base = 500000.0
BF = jnp.bfloat16
F32 = jnp.float32
STRIPS = (5, 3)
HOLD_FLOPS = 4 * 10**10


def after(value, *earlier):
    return lax.optimization_barrier((value,) + earlier)[0]


def hold_kernel(*refs):
    del refs


def hold(value, *earlier):
    anywhere = pl.BlockSpec(memory_space=pl.ANY)
    return pl.pallas_call(
        hold_kernel,
        in_specs=[anywhere] * (1 + len(earlier)),
        out_specs=anywhere,
        out_shape=jax.ShapeDtypeStruct(value.shape, value.dtype),
        input_output_aliases={0: 0},
        cost_estimate=pl.CostEstimate(flops=HOLD_FLOPS, transcendentals=0, bytes_accessed=1024),
        name="hold",
    )(value, *earlier)


def z_route(step, sections, tensors):
    low_count = 4
    rows = sections // low_count
    cores = 2
    high_count = tensors // cores
    depth = low_count * high_count
    route = []
    for z in range(depth):
        origin = (z + step) % depth
        for y in range(rows):
            for core in range(cores):
                source = ((origin % low_count) * rows + y) * tensors + (origin // low_count) * cores + core
                target = ((z % low_count) * rows + y) * tensors + (z // low_count) * cores + core
                route.append((source, target))
    return route


def from_z(block, step):
    route = z_route(step, lax.axis_size("section"), lax.axis_size("tensor"))
    return lax.ppermute(block, ("section", "tensor"), route)


def from_x(block, step):
    count = lax.axis_size("ctx")
    return lax.ppermute(block, "ctx", [((c + step) % count, c) for c in range(count)])


def from_before(block, step):
    count = lax.axis_size("ctx")
    return lax.ppermute(block, "ctx", [(c - step, c) for c in range(step, count)])


def from_tensor(block, flip):
    count = lax.axis_size("tensor")
    return lax.ppermute(block, "tensor", [(t, t ^ flip) for t in range(count)])


def first_hop(shard):
    return from_x(shard, 1), from_x(shard, -1)


def second_hop(ahead, behind):
    half = ahead.shape[0] // 2
    return from_x(ahead[:half], 1), from_x(behind[half:], -1)


def rope_tables(rows):
    half = HEAD // 2
    exponent = jnp.arange(half).astype(F32) * (2.0 / HEAD)
    inverse = jnp.exp(-exponent * math.log(rope_base))
    positions = lax.axis_index("ctx") * rows + jnp.arange(rows, dtype=jnp.int32)
    angles = positions.astype(F32)[:, None] * inverse[None, :]
    cosine = jnp.cos(angles)
    sine = jnp.sin(angles)
    return jnp.concatenate((cosine, cosine), axis=1), jnp.concatenate((-sine, sine), axis=1)


def normalize_kernel(*refs):
    block_refs, gain_ref, out_ref = refs[:8], refs[8], refs[9]
    for batch in range(2):
        blocks = [ref[...].astype(F32) for ref in block_refs[4 * batch : 4 * batch + 4]]
        total = sum(jnp.sum(block * block, axis=1, keepdims=True) for block in blocks)
        scale = lax.rsqrt(total * (1.0 / (blocks[0].shape[1] * len(blocks))) + norm_epsilon)
        for flip, block in enumerate(blocks):
            gain = gain_ref[flip : flip + 1].astype(F32)
            out_ref[flip, batch] = (block * scale * gain).astype(BF)


def normalize(blocks, gains, rows):
    width = gains.shape[1]
    step = 64
    split = [
        pl.BlockSpec((step, width), functools.partial(lambda skip, n: (skip + n, 0), part * (rows // step)))
        for _, part in blocks
    ]
    out = pl.pallas_call(
        normalize_kernel,
        grid=(rows // step,),
        in_specs=split + [pl.BlockSpec(gains.shape, lambda n: (0, 0))],
        out_specs=pl.BlockSpec((4, 2, step, width), lambda n: (0, 0, n, 0)),
        out_shape=jax.ShapeDtypeStruct((4, 2, rows, width), BF),
        compiler_params=pltpu.CompilerParams(vmem_limit_bytes=24 << 20),
        cost_estimate=pl.CostEstimate(flops=1024, transcendentals=0, bytes_accessed=1024),
        name="normalize",
    )(*[array for array, _ in blocks], gains)
    return out.reshape(4, 2 * rows, width)


def project_kernel(index_ref, normed_ref, *refs, pieces, turned):
    piece_refs, (cosine_ref, sine_ref, out_ref) = refs[: len(pieces)], refs[len(pieces) :]
    total = sum(
        jnp.dot(
            normed_ref[index_ref[step], :, low : low + ref.shape[0]], ref[...], preferred_element_type=F32
        )
        for (step, low), ref in zip(pieces, piece_refs)
    )
    for head in range(total.shape[1] // HEAD):
        raw = total[:, head * HEAD : (head + 1) * HEAD]
        if head < turned:
            raw = raw * cosine_ref[...] + pltpu.roll(raw, HEAD // 2, 1) * sine_ref[...]
        out_ref[:, head * HEAD : (head + 1) * HEAD] = raw.astype(BF)


def project(order, normed, shards, cosine, sine, turned, name):
    blocks, tokens, depth = normed.shape
    arrays = [array for array, _, _ in shards]
    columns = arrays[0].shape[1]
    wide = 2 * HEAD
    whole = lambda n, order: (0, 0)
    strip = lambda n, order: (0, n)
    return pl.pallas_call(
        functools.partial(project_kernel, pieces=[(step, low) for _, step, low in shards], turned=turned),
        grid_spec=pltpu.PrefetchScalarGridSpec(
            num_scalar_prefetch=1,
            grid=(columns // wide,),
            in_specs=[pl.BlockSpec((blocks, tokens, depth), lambda n, order: (0, 0, 0))]
            + [pl.BlockSpec((array.shape[0], wide), strip) for array in arrays]
            + [pl.BlockSpec((tokens, HEAD), whole)] * 2,
            out_specs=pl.BlockSpec((tokens, wide), strip),
        ),
        out_shape=jax.ShapeDtypeStruct((tokens, columns), BF),
        compiler_params=pltpu.CompilerParams(vmem_limit_bytes=32 << 20),
        cost_estimate=pl.CostEstimate(flops=1024, transcendentals=0, bytes_accessed=1024),
        name=name,
    )(order, normed, *arrays, cosine, sine)


def attend_kernel(query_ref, key_ref, value_ref, query_doc_ref, key_doc_ref, out_ref, bias_ref):
    rows, span = bias_ref.shape
    back = span - rows

    @pl.when(pl.program_id(1) == 0)
    def _():
        at_query = lax.broadcasted_iota(jnp.int32, (rows, span), 0)
        at_key = lax.broadcasted_iota(jnp.int32, (rows, span), 1) - back
        allowed = (at_key <= at_query) & (query_doc_ref[0] == key_doc_ref[0])
        bias_ref[...] = jnp.where(allowed, 0.0, -jnp.inf)

    for head in range(query_ref.shape[1] // HEAD):
        part = slice(head * HEAD, (head + 1) * HEAD)
        scores = lax.dot_general(
            query_ref[:, part], key_ref[0], (((1,), (1,)), ((), ())), preferred_element_type=F32
        )
        masked = scores + bias_ref[...]
        peak = jnp.max(masked, axis=1, keepdims=True)
        weights = jnp.exp((masked - peak) * (1.0 / math.sqrt(HEAD)))
        totals = jnp.sum(weights, axis=1, keepdims=True)
        mixed = jnp.dot(weights.astype(BF), value_ref[0], preferred_element_type=F32)
        out_ref[:, part] = (mixed / totals).astype(BF)


def attend(queries, pairs, query_docs, key_docs):
    batches, span, _ = pairs.shape
    rows = queries.shape[0] // batches
    wide = 2 * HEAD
    return pl.pallas_call(
        attend_kernel,
        grid=(batches, queries.shape[1] // wide),
        in_specs=[
            pl.BlockSpec((rows, wide), lambda b, h: (b, h)),
            pl.BlockSpec((1, span, HEAD), lambda b, h: (b, 0, 0)),
            pl.BlockSpec((1, span, HEAD), lambda b, h: (b, 0, 1)),
            pl.BlockSpec((1, rows, 1), lambda b, h: (b, 0, 0)),
            pl.BlockSpec((1, 1, span), lambda b, h: (b, 0, 0)),
        ],
        out_specs=pl.BlockSpec((rows, wide), lambda b, h: (b, h)),
        out_shape=jax.ShapeDtypeStruct(queries.shape, BF),
        scratch_shapes=[pltpu.VMEM((rows, span), F32)],
        compiler_params=pltpu.CompilerParams(vmem_limit_bytes=24 << 20),
        cost_estimate=pl.CostEstimate(flops=1024, transcendentals=0, bytes_accessed=1024),
        name="attend",
    )(queries, pairs, pairs, query_docs, key_docs)


def spread_kernel(
    index_ref, mixed_ref, own_ref, ahead_ref, near_ref, back_ref, behind_ref,
    sent_kept_ref, sent_passed_ref, kept_ref, passed_ref, terms_ref,
):
    half = near_ref.shape[0]
    for step, shard in ((0, own_ref), (1, ahead_ref), (3, behind_ref)):
        terms_ref[step] = jnp.dot(mixed_ref[...], shard[...], preferred_element_type=F32)
    terms_ref[2] = jnp.dot(mixed_ref[:, :half], near_ref[...], preferred_element_type=F32) + jnp.dot(
        mixed_ref[:, half:], back_ref[...], preferred_element_type=F32
    )
    sent_kept_ref[...] = terms_ref[index_ref[1]].astype(BF)
    sent_passed_ref[...] = terms_ref[index_ref[3]].astype(BF)
    kept_ref[...] = terms_ref[index_ref[0]]
    passed_ref[...] = terms_ref[index_ref[2]]


def spread(order, mixed, shards, name):
    tokens, _ = mixed.shape
    columns = shards[0].shape[1]
    return pl.pallas_call(
        spread_kernel,
        in_specs=[pl.BlockSpec(memory_space=pltpu.SMEM)] + [pl.BlockSpec(memory_space=pltpu.VMEM)] * 6,
        out_specs=[pl.BlockSpec(memory_space=pltpu.VMEM)] * 4,
        out_shape=[
            jax.ShapeDtypeStruct((tokens, columns), BF),
            jax.ShapeDtypeStruct((tokens, columns), BF),
            jax.ShapeDtypeStruct((tokens, columns), F32),
            jax.ShapeDtypeStruct((tokens, columns), F32),
        ],
        scratch_shapes=[pltpu.VMEM((4, tokens, columns), F32)],
        compiler_params=pltpu.CompilerParams(vmem_limit_bytes=24 << 20),
        cost_estimate=pl.CostEstimate(flops=1024, transcendentals=0, bytes_accessed=1024),
        name=name,
    )(order, mixed, *shards)


def body(
    arriving,
    stored,
    docs_forward,
    docs_backward,
    norm_gain,
    query_weight,
    key_weight,
    value_projection_weight,
    out_weight,
):
    mine = arriving[0]
    held = stored[0]
    rows, width = mine.shape
    ring = lax.axis_size("ctx")
    c = lax.axis_index("ctx")
    t = lax.axis_index("tensor")
    near_high = lax.axis_index("section") < lax.axis_size("section") // 2
    docs = jnp.stack((docs_forward[0], docs_backward[0]), axis=0)
    flips = jnp.arange(4, dtype=jnp.int32)
    half = rows // 2

    strips = []
    start = 0
    for share in STRIPS:
        strips.append((start, start + width * share // sum(STRIPS)))
        start = strips[-1][1]
    out_own = [out_weight[0][:, low:high] for low, high in strips]

    q_weight = query_weight[0]
    depth = q_weight.shape[0] // 2
    with jax.named_scope("q_hop1"):
        q_ahead, q_behind = first_hop(q_weight)
    kv_weight = jnp.concatenate((key_weight[0], value_projection_weight[0]), axis=1)
    with jax.named_scope("kv_hop1"):
        kv_ahead, kv_behind = first_hop(kv_weight)
    both = jnp.concatenate((mine, held), axis=0)
    with jax.named_scope("z_in"):
        up, down = from_z(both, 2), from_z(both, -2)
    q_ahead, q_behind, kv_ahead, kv_behind, up, down, out_own[0] = lax.optimization_barrier(
        (q_ahead, q_behind, kv_ahead, kv_behind, up, down, out_own[0])
    )

    with jax.named_scope("q_hop2"):
        across_low, across_high = second_hop(q_ahead, q_behind)
    with jax.named_scope("kv_hop2"):
        kv_across = from_x(kv_ahead, 1)
    with jax.named_scope("far"):
        mine_far = jnp.concatenate((from_z(up[:half], 2), from_z(down[half:rows], -2)), axis=0)
    stashed = jnp.where(near_high, up[:rows], down[:rows])
    fetched = jnp.where(near_high, up[rows:], down[rows:])
    fetched_far = jnp.where(near_high, down[rows:], up[rows:])
    with jax.named_scope("sib"):
        sib = from_tensor(jnp.concatenate((mine, fetched, fetched_far, mine_far), axis=0), 1)
    blocks = (
        ((mine, 0), (sib, 0), (mine_far, 0), (sib, 3))
        + ((fetched, 0), (sib, 1), (fetched_far, 0), (sib, 2))
    )
    gains = norm_gain[0].reshape(-1, width)
    normed = normalize(blocks, jnp.take(gains, t ^ flips, axis=0), rows)
    cosine, sine = rope_tables(rows)
    cosine, sine = jnp.concatenate((cosine, cosine), axis=0), jnp.concatenate((sine, sine), axis=0)
    feature_order = t ^ ((c + flips) % ring)

    own_kv = project(
        feature_order,
        normed,
        ((kv_weight, 0, 0), (kv_ahead, 1, 0), (kv_across, 2, 0), (kv_behind, 3, 0)),
        cosine,
        sine,
        1,
        "project_kv",
    )
    id_rows = 16
    ids = jnp.broadcast_to(docs.astype(BF)[:, None, :], (2, id_rows, rows))
    own_pair = jnp.concatenate((ids, own_kv.reshape(2, rows, 2 * HEAD)), axis=1)
    with jax.named_scope("kv_rows"):
        kv_one, kv_two = from_before(own_pair, 1), from_before(own_pair, 2)
    with jax.named_scope("out_hop1_0"):
        out_own[0] = hold(out_own[0], across_low, across_high, kv_across)
        out_hops = [first_hop(out_own[0])]
    all_kv = jnp.concatenate((kv_two[:, id_rows:], kv_one[:, id_rows:], own_pair[:, id_rows:]), axis=1)
    docs_one = jnp.where(c >= 1, kv_one[:, 0].astype(jnp.int32), -1)
    docs_two = jnp.where(c >= 2, kv_two[:, 0].astype(jnp.int32), -1)
    key_docs = jnp.concatenate((docs_two, docs_one, docs), axis=1)
    queries = project(
        feature_order,
        after(normed, own_kv),
        (
            (q_weight, 0, 0),
            (q_ahead, 1, 0),
            (q_behind, 3, 0),
            (across_low, 2, 0),
            (across_high, 2, depth),
        ),
        cosine,
        sine,
        2,
        "project_q",
    )
    queries, out_own[1] = lax.optimization_barrier((queries, out_own[1]))
    mixed = attend(queries, all_kv, docs[:, :, None], key_docs[:, None, :])

    residual = jnp.concatenate((mine, fetched), axis=0)
    term_order = ((t ^ flips) - c) % ring
    passed_before = []
    outputs = []
    for index, (low, high) in enumerate(strips):
        ahead, behind = out_hops[index]
        with jax.named_scope("out_hop2_%d" % index):
            near, back = second_hop(ahead, behind)
        if index + 1 < len(strips):
            with jax.named_scope("out_hop1_%d" % (index + 1)):
                out_hops.append(first_hop(after(out_own[index + 1], near, back)))
        sent_kept, sent_passed, kept, passed = spread(
            term_order,
            after(mixed, *passed_before),
            (out_own[index], ahead, near, back, behind),
            "spread_%d" % index,
        )
        if index:
            sent_passed = after(sent_passed, outputs[-1])
        with jax.named_scope("core_passed_%d" % index):
            passed = (passed + from_tensor(sent_passed, 1).astype(F32)).astype(BF)
        with jax.named_scope("z_sum_%d" % index):
            arrived = from_tensor(passed, 2)
        with jax.named_scope("core_kept_%d" % index):
            kept = kept + from_tensor(sent_kept, 1).astype(F32)
        passed_before = [passed]
        base = residual[:, low:high].astype(F32)
        outputs.append((base + (kept + arrived.astype(F32))).astype(BF))
    result = jnp.concatenate(outputs, axis=1)
    return (result[:rows][None], stashed[None], result[rows:][None])


def solution(mesh):
    return jax.shard_map(
        body,
        mesh=mesh,
        in_specs=(
            P("section", "ctx", "tensor"),
            P("section", "ctx", "tensor"),
            P("section", "ctx"),
            P("section", "ctx"),
            P("section", None),
            P("section", "ctx", "tensor"),
            P("section", "ctx", "tensor"),
            P("section", "ctx", "tensor"),
            P("section", "tensor", "ctx"),
        ),
        out_specs=(
            P("section", "ctx", "tensor"),
            P("section", "ctx", "tensor"),
            P("section", "ctx", "tensor"),
        ),
        check_vma=False,
    )
```

```python
import functools
import math

import jax
import jax.numpy as jnp
from jax import lax
from jax.experimental import pallas as pl
from jax.experimental.pallas import tpu as pltpu
from jax.sharding import PartitionSpec as P

HEAD = 128
norm_epsilon = 1e-05
rope_base = 500000.0
BF = jnp.bfloat16
F32 = jnp.float32
STRIPS = (5, 3)
SHORT = 10**10
LONG = 4 * 10**10


def after(value, *earlier):
    return lax.optimization_barrier((value,) + earlier)[0]


def hold_kernel(*refs):
    del refs


def hold(value, *earlier, flops):
    anywhere = pl.BlockSpec(memory_space=pl.ANY)
    return pl.pallas_call(
        hold_kernel,
        in_specs=[anywhere] * (1 + len(earlier)),
        out_specs=anywhere,
        out_shape=jax.ShapeDtypeStruct(value.shape, value.dtype),
        input_output_aliases={0: 0},
        cost_estimate=pl.CostEstimate(flops=flops, transcendentals=0, bytes_accessed=1024),
        name="hold",
    )(value, *earlier)


def z_route(step, sections, tensors):
    low_count = 4
    rows = sections // low_count
    cores = 2
    high_count = tensors // cores
    depth = low_count * high_count
    route = []
    for z in range(depth):
        origin = (z + step) % depth
        for y in range(rows):
            for core in range(cores):
                source = ((origin % low_count) * rows + y) * tensors + (origin // low_count) * cores + core
                target = ((z % low_count) * rows + y) * tensors + (z // low_count) * cores + core
                route.append((source, target))
    return route


def from_z(block, step):
    route = z_route(step, lax.axis_size("section"), lax.axis_size("tensor"))
    return lax.ppermute(block, ("section", "tensor"), route)


def from_x(block, step):
    count = lax.axis_size("ctx")
    return lax.ppermute(block, "ctx", [((c + step) % count, c) for c in range(count)])


def from_before(block, step):
    count = lax.axis_size("ctx")
    return lax.ppermute(block, "ctx", [(c - step, c) for c in range(step, count)])


def from_tensor(block, flip):
    count = lax.axis_size("tensor")
    return lax.ppermute(block, "tensor", [(t, t ^ flip) for t in range(count)])


def first_hop(shard):
    return from_x(shard, 1), from_x(shard, -1)


def second_hop(ahead, behind):
    half = ahead.shape[0] // 2
    return from_x(ahead[:half], 1), from_x(behind[half:], -1)


def rope_tables(rows):
    half = HEAD // 2
    exponent = jnp.arange(half).astype(F32) * (2.0 / HEAD)
    inverse = jnp.exp(-exponent * math.log(rope_base))
    positions = lax.axis_index("ctx") * rows + jnp.arange(rows, dtype=jnp.int32)
    angles = positions.astype(F32)[:, None] * inverse[None, :]
    cosine = jnp.cos(angles)
    sine = jnp.sin(angles)
    return jnp.concatenate((cosine, cosine), axis=1), jnp.concatenate((-sine, sine), axis=1)


def normalize_kernel(*refs):
    block_refs, gain_ref, out_ref = refs[:8], refs[8], refs[9]
    for batch in range(2):
        blocks = [ref[...].astype(F32) for ref in block_refs[4 * batch : 4 * batch + 4]]
        total = sum(jnp.sum(block * block, axis=1, keepdims=True) for block in blocks)
        scale = lax.rsqrt(total * (1.0 / (blocks[0].shape[1] * len(blocks))) + norm_epsilon)
        for flip, block in enumerate(blocks):
            gain = gain_ref[flip : flip + 1].astype(F32)
            out_ref[flip, batch] = (block * scale * gain).astype(BF)


def normalize(blocks, gains, rows):
    width = gains.shape[1]
    step = 64
    split = [
        pl.BlockSpec((step, width), functools.partial(lambda skip, n: (skip + n, 0), part * (rows // step)))
        for _, part in blocks
    ]
    out = pl.pallas_call(
        normalize_kernel,
        grid=(rows // step,),
        in_specs=split + [pl.BlockSpec(gains.shape, lambda n: (0, 0))],
        out_specs=pl.BlockSpec((4, 2, step, width), lambda n: (0, 0, n, 0)),
        out_shape=jax.ShapeDtypeStruct((4, 2, rows, width), BF),
        compiler_params=pltpu.CompilerParams(vmem_limit_bytes=24 << 20),
        cost_estimate=pl.CostEstimate(flops=1024, transcendentals=0, bytes_accessed=1024),
        name="normalize",
    )(*[array for array, _ in blocks], gains)
    return out.reshape(4, 2 * rows, width)


def project_kernel(index_ref, normed_ref, *refs, pieces, turned):
    piece_refs, (cosine_ref, sine_ref, out_ref) = refs[: len(pieces)], refs[len(pieces) :]
    total = sum(
        jnp.dot(
            normed_ref[index_ref[step], :, low : low + ref.shape[0]], ref[...], preferred_element_type=F32
        )
        for (step, low), ref in zip(pieces, piece_refs)
    )
    for head in range(total.shape[1] // HEAD):
        raw = total[:, head * HEAD : (head + 1) * HEAD]
        if head < turned:
            raw = raw * cosine_ref[...] + pltpu.roll(raw, HEAD // 2, 1) * sine_ref[...]
        out_ref[:, head * HEAD : (head + 1) * HEAD] = raw.astype(BF)


def project(order, normed, shards, cosine, sine, turned, name):
    blocks, tokens, depth = normed.shape
    arrays = [array for array, _, _ in shards]
    columns = arrays[0].shape[1]
    wide = 2 * HEAD
    whole = lambda n, order: (0, 0)
    strip = lambda n, order: (0, n)
    return pl.pallas_call(
        functools.partial(project_kernel, pieces=[(step, low) for _, step, low in shards], turned=turned),
        grid_spec=pltpu.PrefetchScalarGridSpec(
            num_scalar_prefetch=1,
            grid=(columns // wide,),
            in_specs=[pl.BlockSpec((blocks, tokens, depth), lambda n, order: (0, 0, 0))]
            + [pl.BlockSpec((array.shape[0], wide), strip) for array in arrays]
            + [pl.BlockSpec((tokens, HEAD), whole)] * 2,
            out_specs=pl.BlockSpec((tokens, wide), strip),
        ),
        out_shape=jax.ShapeDtypeStruct((tokens, columns), BF),
        compiler_params=pltpu.CompilerParams(vmem_limit_bytes=32 << 20),
        cost_estimate=pl.CostEstimate(flops=1024, transcendentals=0, bytes_accessed=1024),
        name=name,
    )(order, normed, *arrays, cosine, sine)


def attend_kernel(query_ref, key_ref, value_ref, query_doc_ref, key_doc_ref, out_ref, bias_ref):
    rows, span = bias_ref.shape
    back = span - rows

    @pl.when(pl.program_id(1) == 0)
    def _():
        at_query = lax.broadcasted_iota(jnp.int32, (rows, span), 0)
        at_key = lax.broadcasted_iota(jnp.int32, (rows, span), 1) - back
        allowed = (at_key <= at_query) & (query_doc_ref[0] == key_doc_ref[0])
        bias_ref[...] = jnp.where(allowed, 0.0, -jnp.inf)

    for head in range(query_ref.shape[1] // HEAD):
        part = slice(head * HEAD, (head + 1) * HEAD)
        scores = lax.dot_general(
            query_ref[:, part], key_ref[0], (((1,), (1,)), ((), ())), preferred_element_type=F32
        )
        masked = scores + bias_ref[...]
        peak = jnp.max(masked, axis=1, keepdims=True)
        weights = jnp.exp((masked - peak) * (1.0 / math.sqrt(HEAD)))
        totals = jnp.sum(weights, axis=1, keepdims=True)
        mixed = jnp.dot(weights.astype(BF), value_ref[0], preferred_element_type=F32)
        out_ref[:, part] = (mixed / totals).astype(BF)


def attend(queries, pairs, query_docs, key_docs):
    batches, span, _ = pairs.shape
    rows = queries.shape[0] // batches
    wide = 2 * HEAD
    return pl.pallas_call(
        attend_kernel,
        grid=(batches, queries.shape[1] // wide),
        in_specs=[
            pl.BlockSpec((rows, wide), lambda b, h: (b, h)),
            pl.BlockSpec((1, span, HEAD), lambda b, h: (b, 0, 0)),
            pl.BlockSpec((1, span, HEAD), lambda b, h: (b, 0, 1)),
            pl.BlockSpec((1, rows, 1), lambda b, h: (b, 0, 0)),
            pl.BlockSpec((1, 1, span), lambda b, h: (b, 0, 0)),
        ],
        out_specs=pl.BlockSpec((rows, wide), lambda b, h: (b, h)),
        out_shape=jax.ShapeDtypeStruct(queries.shape, BF),
        scratch_shapes=[pltpu.VMEM((rows, span), F32)],
        compiler_params=pltpu.CompilerParams(vmem_limit_bytes=24 << 20),
        cost_estimate=pl.CostEstimate(flops=1024, transcendentals=0, bytes_accessed=1024),
        name="attend",
    )(queries, pairs, pairs, query_docs, key_docs)


def spread_kernel(
    index_ref, mixed_ref, own_ref, ahead_ref, near_ref, back_ref, behind_ref,
    sent_kept_ref, sent_passed_ref, kept_ref, passed_ref, terms_ref,
):
    half = near_ref.shape[0]
    for step, shard in ((0, own_ref), (1, ahead_ref), (3, behind_ref)):
        terms_ref[step] = jnp.dot(mixed_ref[...], shard[...], preferred_element_type=F32)
    terms_ref[2] = jnp.dot(mixed_ref[:, :half], near_ref[...], preferred_element_type=F32) + jnp.dot(
        mixed_ref[:, half:], back_ref[...], preferred_element_type=F32
    )
    sent_kept_ref[...] = terms_ref[index_ref[1]].astype(BF)
    sent_passed_ref[...] = terms_ref[index_ref[3]].astype(BF)
    kept_ref[...] = terms_ref[index_ref[0]]
    passed_ref[...] = terms_ref[index_ref[2]]


def spread(order, mixed, shards, name):
    tokens, _ = mixed.shape
    columns = shards[0].shape[1]
    return pl.pallas_call(
        spread_kernel,
        in_specs=[pl.BlockSpec(memory_space=pltpu.SMEM)] + [pl.BlockSpec(memory_space=pltpu.VMEM)] * 6,
        out_specs=[pl.BlockSpec(memory_space=pltpu.VMEM)] * 4,
        out_shape=[
            jax.ShapeDtypeStruct((tokens, columns), BF),
            jax.ShapeDtypeStruct((tokens, columns), BF),
            jax.ShapeDtypeStruct((tokens, columns), F32),
            jax.ShapeDtypeStruct((tokens, columns), F32),
        ],
        scratch_shapes=[pltpu.VMEM((4, tokens, columns), F32)],
        compiler_params=pltpu.CompilerParams(vmem_limit_bytes=24 << 20),
        cost_estimate=pl.CostEstimate(flops=1024, transcendentals=0, bytes_accessed=1024),
        name=name,
    )(order, mixed, *shards)


def body(
    arriving,
    stored,
    docs_forward,
    docs_backward,
    norm_gain,
    query_weight,
    key_weight,
    value_projection_weight,
    out_weight,
):
    mine = arriving[0]
    held = stored[0]
    rows, width = mine.shape
    ring = lax.axis_size("ctx")
    c = lax.axis_index("ctx")
    t = lax.axis_index("tensor")
    near_high = lax.axis_index("section") < lax.axis_size("section") // 2
    docs = jnp.stack((docs_forward[0], docs_backward[0]), axis=0)
    flips = jnp.arange(4, dtype=jnp.int32)
    half = rows // 2

    strips = []
    start = 0
    for share in STRIPS:
        strips.append((start, start + width * share // sum(STRIPS)))
        start = strips[-1][1]
    out_own = [out_weight[0][:, low:high] for low, high in strips]

    q_weight = query_weight[0]
    depth = q_weight.shape[0] // 2
    with jax.named_scope("q_hop1"):
        q_ahead, q_behind = first_hop(q_weight)
    kv_weight = jnp.concatenate((key_weight[0], value_projection_weight[0]), axis=1)
    with jax.named_scope("kv_hop1"):
        kv_ahead, kv_behind = first_hop(after(kv_weight, q_ahead, q_behind))
    both = jnp.concatenate((mine, held), axis=0)
    with jax.named_scope("z_in"):
        up, down = from_z(both, 2), from_z(both, -2)
        up = hold(up, down, flops=SHORT)
    q_ahead, q_behind, kv_ahead, kv_behind, up, down, out_own[0] = lax.optimization_barrier(
        (q_ahead, q_behind, kv_ahead, kv_behind, up, down, out_own[0])
    )

    with jax.named_scope("q_hop2"):
        across_low, across_high = second_hop(q_ahead, q_behind)
    with jax.named_scope("kv_hop2"):
        kv_near, kv_back = second_hop(kv_ahead, kv_behind)
    with jax.named_scope("far"):
        mine_far = jnp.concatenate((from_z(up[:half], 2), from_z(down[half:rows], -2)), axis=0)
    stashed = jnp.where(near_high, up[:rows], down[:rows])
    fetched = jnp.where(near_high, up[rows:], down[rows:])
    fetched_far = jnp.where(near_high, down[rows:], up[rows:])
    with jax.named_scope("sib"):
        sib = from_tensor(jnp.concatenate((mine, fetched, fetched_far, mine_far), axis=0), 1)
    blocks = (
        ((mine, 0), (sib, 0), (mine_far, 0), (sib, 3))
        + ((fetched, 0), (sib, 1), (fetched_far, 0), (sib, 2))
    )
    gains = norm_gain[0].reshape(-1, width)
    normed = normalize(blocks, jnp.take(gains, t ^ flips, axis=0), rows)
    cosine, sine = rope_tables(rows)
    cosine, sine = jnp.concatenate((cosine, cosine), axis=0), jnp.concatenate((sine, sine), axis=0)
    feature_order = t ^ ((c + flips) % ring)

    own_kv = project(
        feature_order,
        normed,
        ((kv_weight, 0, 0), (kv_ahead, 1, 0), (kv_near, 2, 0), (kv_back, 2, depth), (kv_behind, 3, 0)),
        cosine,
        sine,
        1,
        "project_kv",
    )
    id_rows = 16
    ids = jnp.broadcast_to(docs.astype(BF)[:, None, :], (2, id_rows, rows))
    own_pair = jnp.concatenate((ids, own_kv.reshape(2, rows, 2 * HEAD)), axis=1)
    with jax.named_scope("kv_rows"):
        kv_one, kv_two = from_before(own_pair, 1), from_before(own_pair, 2)
    with jax.named_scope("out_hop1_0"):
        out_own[0] = hold(out_own[0], across_low, across_high, kv_near, kv_back, flops=LONG)
        out_hops = [first_hop(out_own[0])]
    all_kv = jnp.concatenate((kv_two[:, id_rows:], kv_one[:, id_rows:], own_pair[:, id_rows:]), axis=1)
    docs_one = jnp.where(c >= 1, kv_one[:, 0].astype(jnp.int32), -1)
    docs_two = jnp.where(c >= 2, kv_two[:, 0].astype(jnp.int32), -1)
    key_docs = jnp.concatenate((docs_two, docs_one, docs), axis=1)
    queries = project(
        feature_order,
        after(normed, own_kv),
        (
            (q_weight, 0, 0),
            (q_ahead, 1, 0),
            (q_behind, 3, 0),
            (across_low, 2, 0),
            (across_high, 2, depth),
        ),
        cosine,
        sine,
        2,
        "project_q",
    )
    queries, out_own[1] = lax.optimization_barrier((queries, out_own[1]))
    mixed = attend(queries, all_kv, docs[:, :, None], key_docs[:, None, :])

    residual = jnp.concatenate((mine, fetched), axis=0)
    term_order = ((t ^ flips) - c) % ring
    passed_before = []
    outputs = []
    for index, (low, high) in enumerate(strips):
        ahead, behind = out_hops[index]
        with jax.named_scope("out_hop2_%d" % index):
            near, back = second_hop(ahead, behind)
        if index + 1 < len(strips):
            with jax.named_scope("out_hop1_%d" % (index + 1)):
                out_hops.append(first_hop(after(out_own[index + 1], near, back)))
        sent_kept, sent_passed, kept, passed = spread(
            term_order,
            after(mixed, *passed_before),
            (out_own[index], ahead, near, back, behind),
            "spread_%d" % index,
        )
        if index:
            sent_passed = after(sent_passed, outputs[-1])
        with jax.named_scope("core_passed_%d" % index):
            passed = (passed + from_tensor(sent_passed, 1).astype(F32)).astype(BF)
        with jax.named_scope("z_sum_%d" % index):
            arrived = from_tensor(passed, 2)
        with jax.named_scope("core_kept_%d" % index):
            kept = kept + from_tensor(sent_kept, 1).astype(F32)
        passed_before = [passed]
        base = residual[:, low:high].astype(F32)
        outputs.append((base + (kept + arrived.astype(F32))).astype(BF))
    result = jnp.concatenate(outputs, axis=1)
    return (result[:rows][None], stashed[None], result[rows:][None])


def solution(mesh):
    return jax.shard_map(
        body,
        mesh=mesh,
        in_specs=(
            P("section", "ctx", "tensor"),
            P("section", "ctx", "tensor"),
            P("section", "ctx"),
            P("section", "ctx"),
            P("section", None),
            P("section", "ctx", "tensor"),
            P("section", "ctx", "tensor"),
            P("section", "ctx", "tensor"),
            P("section", "tensor", "ctx"),
        ),
        out_specs=(
            P("section", "ctx", "tensor"),
            P("section", "ctx", "tensor"),
            P("section", "ctx", "tensor"),
        ),
        check_vma=False,
    )
```

```python
import functools
import math

import jax
import jax.numpy as jnp
from jax import lax
from jax.experimental import pallas as pl
from jax.experimental.pallas import tpu as pltpu
from jax.sharding import PartitionSpec as P

HEAD = 128
norm_epsilon = 1e-05
rope_base = 500000.0
BF = jnp.bfloat16
F32 = jnp.float32
STRIPS = (1, 1)
SHORT = 10**10
LONG = 4 * 10**10


def after(value, *earlier):
    return lax.optimization_barrier((value,) + earlier)[0]


def hold_kernel(*refs):
    del refs


def hold(value, *earlier, flops):
    anywhere = pl.BlockSpec(memory_space=pl.ANY)
    return pl.pallas_call(
        hold_kernel,
        in_specs=[anywhere] * (1 + len(earlier)),
        out_specs=anywhere,
        out_shape=jax.ShapeDtypeStruct(value.shape, value.dtype),
        input_output_aliases={0: 0},
        cost_estimate=pl.CostEstimate(flops=flops, transcendentals=0, bytes_accessed=1024),
        name="hold",
    )(value, *earlier)


def z_route(step, sections, tensors):
    low_count = 4
    rows = sections // low_count
    cores = 2
    high_count = tensors // cores
    depth = low_count * high_count
    route = []
    for z in range(depth):
        origin = (z + step) % depth
        for y in range(rows):
            for core in range(cores):
                source = ((origin % low_count) * rows + y) * tensors + (origin // low_count) * cores + core
                target = ((z % low_count) * rows + y) * tensors + (z // low_count) * cores + core
                route.append((source, target))
    return route


def from_z(block, step):
    route = z_route(step, lax.axis_size("section"), lax.axis_size("tensor"))
    return lax.ppermute(block, ("section", "tensor"), route)


def from_x(block, step):
    count = lax.axis_size("ctx")
    return lax.ppermute(block, "ctx", [((c + step) % count, c) for c in range(count)])


def from_before(block, step):
    count = lax.axis_size("ctx")
    return lax.ppermute(block, "ctx", [(c - step, c) for c in range(step, count)])


def from_tensor(block, flip):
    count = lax.axis_size("tensor")
    return lax.ppermute(block, "tensor", [(t, t ^ flip) for t in range(count)])


def first_hop(shard):
    return from_x(shard, 1), from_x(shard, -1)


def second_hop(ahead, behind):
    half = ahead.shape[0] // 2
    return from_x(ahead[:half], 1), from_x(behind[half:], -1)


def rope_tables(rows):
    half = HEAD // 2
    exponent = jnp.arange(half).astype(F32) * (2.0 / HEAD)
    inverse = jnp.exp(-exponent * math.log(rope_base))
    positions = lax.axis_index("ctx") * rows + jnp.arange(rows, dtype=jnp.int32)
    angles = positions.astype(F32)[:, None] * inverse[None, :]
    cosine = jnp.cos(angles)
    sine = jnp.sin(angles)
    return jnp.concatenate((cosine, cosine), axis=1), jnp.concatenate((-sine, sine), axis=1)


def normalize_kernel(*refs):
    block_refs, gain_ref, out_ref = refs[:8], refs[8], refs[9]
    for batch in range(2):
        blocks = [ref[...].astype(F32) for ref in block_refs[4 * batch : 4 * batch + 4]]
        total = sum(jnp.sum(block * block, axis=1, keepdims=True) for block in blocks)
        scale = lax.rsqrt(total * (1.0 / (blocks[0].shape[1] * len(blocks))) + norm_epsilon)
        for flip, block in enumerate(blocks):
            gain = gain_ref[flip : flip + 1].astype(F32)
            out_ref[flip, batch] = (block * scale * gain).astype(BF)


def normalize(blocks, gains, rows):
    width = gains.shape[1]
    step = 64
    split = [
        pl.BlockSpec((step, width), functools.partial(lambda skip, n: (skip + n, 0), part * (rows // step)))
        for _, part in blocks
    ]
    out = pl.pallas_call(
        normalize_kernel,
        grid=(rows // step,),
        in_specs=split + [pl.BlockSpec(gains.shape, lambda n: (0, 0))],
        out_specs=pl.BlockSpec((4, 2, step, width), lambda n: (0, 0, n, 0)),
        out_shape=jax.ShapeDtypeStruct((4, 2, rows, width), BF),
        compiler_params=pltpu.CompilerParams(vmem_limit_bytes=24 << 20),
        cost_estimate=pl.CostEstimate(flops=1024, transcendentals=0, bytes_accessed=1024),
        name="normalize",
    )(*[array for array, _ in blocks], gains)
    return out.reshape(4, 2 * rows, width)


def project_kernel(index_ref, normed_ref, *refs, pieces, turned):
    piece_refs, (cosine_ref, sine_ref, out_ref) = refs[: len(pieces)], refs[len(pieces) :]
    total = sum(
        jnp.dot(
            normed_ref[index_ref[step], :, low : low + ref.shape[0]], ref[...], preferred_element_type=F32
        )
        for (step, low), ref in zip(pieces, piece_refs)
    )
    for head in range(total.shape[1] // HEAD):
        raw = total[:, head * HEAD : (head + 1) * HEAD]
        if head < turned:
            raw = raw * cosine_ref[...] + pltpu.roll(raw, HEAD // 2, 1) * sine_ref[...]
        out_ref[:, head * HEAD : (head + 1) * HEAD] = raw.astype(BF)


def project(order, normed, shards, cosine, sine, turned, name):
    blocks, tokens, depth = normed.shape
    arrays = [array for array, _, _ in shards]
    columns = arrays[0].shape[1]
    wide = 2 * HEAD
    whole = lambda n, order: (0, 0)
    strip = lambda n, order: (0, n)
    return pl.pallas_call(
        functools.partial(project_kernel, pieces=[(step, low) for _, step, low in shards], turned=turned),
        grid_spec=pltpu.PrefetchScalarGridSpec(
            num_scalar_prefetch=1,
            grid=(columns // wide,),
            in_specs=[pl.BlockSpec((blocks, tokens, depth), lambda n, order: (0, 0, 0))]
            + [pl.BlockSpec((array.shape[0], wide), strip) for array in arrays]
            + [pl.BlockSpec((tokens, HEAD), whole)] * 2,
            out_specs=pl.BlockSpec((tokens, wide), strip),
        ),
        out_shape=jax.ShapeDtypeStruct((tokens, columns), BF),
        compiler_params=pltpu.CompilerParams(vmem_limit_bytes=32 << 20),
        cost_estimate=pl.CostEstimate(flops=1024, transcendentals=0, bytes_accessed=1024),
        name=name,
    )(order, normed, *arrays, cosine, sine)


def attend_kernel(
    place_ref, query_ref, query_doc_ref, two_ref, one_ref, own_ref, out_ref, bias_ref, key_scratch, value_scratch
):
    rows, span = bias_ref.shape
    back = span - rows

    @pl.when(pl.program_id(1) == 0)
    def _():
        at_query = lax.broadcasted_iota(jnp.int32, (rows, rows), 0)
        at_key = lax.broadcasted_iota(jnp.int32, (rows, rows), 1)
        query_docs = query_doc_ref[0]
        for part, ref in enumerate((two_ref, one_ref, own_ref)):
            place = slice(part * rows, (part + 1) * rows)
            first = ref.shape[1] - rows
            key_scratch[place] = ref[0, first:, :HEAD]
            value_scratch[place] = ref[0, first:, HEAD:]
            exists = place_ref[0] >= 2 - part
            key_docs = jnp.where(exists, ref[0, 0:1, :].astype(F32), -1.0)
            allowed = (at_key + (part * rows - back) <= at_query) & (query_docs == key_docs)
            bias_ref[:, place] = jnp.where(allowed, 0.0, -jnp.inf)

    for head in range(query_ref.shape[1] // HEAD):
        part = slice(head * HEAD, (head + 1) * HEAD)
        scores = lax.dot_general(
            query_ref[:, part], key_scratch[...], (((1,), (1,)), ((), ())), preferred_element_type=F32
        )
        masked = scores + bias_ref[...]
        peak = jnp.max(masked, axis=1, keepdims=True)
        weights = jnp.exp((masked - peak) * (1.0 / math.sqrt(HEAD)))
        totals = jnp.sum(weights, axis=1, keepdims=True)
        mixed = jnp.dot(weights.astype(BF), value_scratch[...], preferred_element_type=F32)
        out_ref[:, part] = (mixed / totals).astype(BF)


def attend(place, queries, query_docs, two, one, own):
    batches, rows, _ = query_docs.shape
    span = 3 * rows
    wide = 2 * HEAD
    pair = pl.BlockSpec((1,) + own.shape[1:], lambda b, h: (b, 0, 0))
    return pl.pallas_call(
        attend_kernel,
        grid=(batches, queries.shape[1] // wide),
        in_specs=[
            pl.BlockSpec(memory_space=pltpu.SMEM),
            pl.BlockSpec((rows, wide), lambda b, h: (b, h)),
            pl.BlockSpec((1, rows, 1), lambda b, h: (b, 0, 0)),
            pair,
            pair,
            pair,
        ],
        out_specs=pl.BlockSpec((rows, wide), lambda b, h: (b, h)),
        out_shape=jax.ShapeDtypeStruct(queries.shape, BF),
        scratch_shapes=[pltpu.VMEM((rows, span), F32), pltpu.VMEM((span, HEAD), BF), pltpu.VMEM((span, HEAD), BF)],
        compiler_params=pltpu.CompilerParams(vmem_limit_bytes=24 << 20),
        cost_estimate=pl.CostEstimate(flops=1024, transcendentals=0, bytes_accessed=1024),
        name="attend",
    )(place, queries, query_docs, two, one, own)


def spread_kernel(
    index_ref, mixed_ref, own_ref, ahead_ref, near_ref, back_ref, behind_ref,
    sent_kept_ref, sent_passed_ref, kept_ref, passed_ref, terms_ref,
):
    half = near_ref.shape[0]
    for step, shard in ((0, own_ref), (1, ahead_ref), (3, behind_ref)):
        terms_ref[step] = jnp.dot(mixed_ref[...], shard[...], preferred_element_type=F32)
    terms_ref[2] = jnp.dot(mixed_ref[:, :half], near_ref[...], preferred_element_type=F32) + jnp.dot(
        mixed_ref[:, half:], back_ref[...], preferred_element_type=F32
    )
    sent_kept_ref[...] = terms_ref[index_ref[1]].astype(BF)
    sent_passed_ref[...] = terms_ref[index_ref[3]].astype(BF)
    kept_ref[...] = terms_ref[index_ref[0]]
    passed_ref[...] = terms_ref[index_ref[2]]


def spread(order, mixed, shards, name):
    tokens, _ = mixed.shape
    columns = shards[0].shape[1]
    return pl.pallas_call(
        spread_kernel,
        in_specs=[pl.BlockSpec(memory_space=pltpu.SMEM)] + [pl.BlockSpec(memory_space=pltpu.VMEM)] * 6,
        out_specs=[pl.BlockSpec(memory_space=pltpu.VMEM)] * 4,
        out_shape=[
            jax.ShapeDtypeStruct((tokens, columns), BF),
            jax.ShapeDtypeStruct((tokens, columns), BF),
            jax.ShapeDtypeStruct((tokens, columns), F32),
            jax.ShapeDtypeStruct((tokens, columns), F32),
        ],
        scratch_shapes=[pltpu.VMEM((4, tokens, columns), F32)],
        compiler_params=pltpu.CompilerParams(vmem_limit_bytes=24 << 20),
        cost_estimate=pl.CostEstimate(flops=1024, transcendentals=0, bytes_accessed=1024),
        name=name,
    )(order, mixed, *shards)


def body(
    arriving,
    stored,
    docs_forward,
    docs_backward,
    norm_gain,
    query_weight,
    key_weight,
    value_projection_weight,
    out_weight,
):
    mine = arriving[0]
    held = stored[0]
    rows, width = mine.shape
    ring = lax.axis_size("ctx")
    c = lax.axis_index("ctx")
    t = lax.axis_index("tensor")
    near_high = lax.axis_index("section") < lax.axis_size("section") // 2
    docs = jnp.stack((docs_forward[0], docs_backward[0]), axis=0)
    flips = jnp.arange(4, dtype=jnp.int32)
    half = rows // 2

    strips = []
    start = 0
    for share in STRIPS:
        strips.append((start, start + width * share // sum(STRIPS)))
        start = strips[-1][1]
    out_own = [out_weight[0][:, low:high] for low, high in strips]

    q_weight = query_weight[0]
    depth = q_weight.shape[0] // 2
    with jax.named_scope("q_hop1"):
        q_ahead, q_behind = first_hop(q_weight)
    kv_weight = jnp.concatenate((key_weight[0], value_projection_weight[0]), axis=1)
    with jax.named_scope("kv_hop1"):
        kv_ahead, kv_behind = first_hop(after(kv_weight, q_ahead, q_behind))
    both = jnp.concatenate((mine, held), axis=0)
    with jax.named_scope("z_in"):
        up, down = from_z(both, 2), from_z(both, -2)
        up = hold(up, down, flops=SHORT)
    q_ahead, q_behind, kv_ahead, kv_behind, up, down, out_own[0] = lax.optimization_barrier(
        (q_ahead, q_behind, kv_ahead, kv_behind, up, down, out_own[0])
    )

    with jax.named_scope("q_hop2"):
        across_low, across_high = second_hop(q_ahead, q_behind)
    with jax.named_scope("kv_hop2"):
        kv_near, kv_back = second_hop(kv_ahead, kv_behind)
    with jax.named_scope("far"):
        mine_far = jnp.concatenate((from_z(up[:half], 2), from_z(down[half:rows], -2)), axis=0)
    stashed = jnp.where(near_high, up[:rows], down[:rows])
    fetched = jnp.where(near_high, up[rows:], down[rows:])
    fetched_far = jnp.where(near_high, down[rows:], up[rows:])
    with jax.named_scope("sib"):
        sib = from_tensor(jnp.concatenate((mine, fetched, fetched_far, mine_far), axis=0), 1)
    blocks = (
        ((mine, 0), (sib, 0), (mine_far, 0), (sib, 3))
        + ((fetched, 0), (sib, 1), (fetched_far, 0), (sib, 2))
    )
    gains = norm_gain[0].reshape(-1, width)
    normed = normalize(blocks, jnp.take(gains, t ^ flips, axis=0), rows)
    cosine, sine = rope_tables(rows)
    cosine, sine = jnp.concatenate((cosine, cosine), axis=0), jnp.concatenate((sine, sine), axis=0)
    feature_order = t ^ ((c + flips) % ring)

    own_kv = project(
        feature_order,
        normed,
        ((kv_weight, 0, 0), (kv_ahead, 1, 0), (kv_near, 2, 0), (kv_back, 2, depth), (kv_behind, 3, 0)),
        cosine,
        sine,
        1,
        "project_kv",
    )
    id_rows = 16
    ids = jnp.broadcast_to(docs.astype(BF)[:, None, :], (2, id_rows, rows))
    own_pair = jnp.concatenate((ids, own_kv.reshape(2, rows, 2 * HEAD)), axis=1)
    with jax.named_scope("kv_rows"):
        kv_one, kv_two = from_before(own_pair, 1), from_before(own_pair, 2)
    with jax.named_scope("out_hop1_0"):
        out_own[0] = hold(out_own[0], across_low, across_high, kv_near, kv_back, flops=LONG)
        out_hops = [first_hop(out_own[0])]
    queries = project(
        feature_order,
        after(normed, own_kv),
        (
            (q_weight, 0, 0),
            (q_ahead, 1, 0),
            (q_behind, 3, 0),
            (across_low, 2, 0),
            (across_high, 2, depth),
        ),
        cosine,
        sine,
        2,
        "project_q",
    )
    queries, out_own[1] = lax.optimization_barrier((queries, out_own[1]))
    kv_one = hold(kv_one, kv_two, queries, flops=SHORT)
    mixed = attend(c.reshape(1), queries, docs.astype(F32)[:, :, None], kv_two, kv_one, own_pair)

    residual = jnp.concatenate((mine, fetched), axis=0)
    term_order = ((t ^ flips) - c) % ring
    passed_before = []
    outputs = []
    for index, (low, high) in enumerate(strips):
        ahead, behind = out_hops[index]
        with jax.named_scope("out_hop2_%d" % index):
            ahead_part, behind_part = ahead[: width // 2], behind[width // 2 :]
            near, back = from_x(ahead_part, 1), from_x(behind_part, -1)
        if index:
            near = hold(near, back, flops=10000000000)
        if index + 1 < len(strips):
            with jax.named_scope("out_hop1_%d" % (index + 1)):
                out_hops.append(first_hop(after(out_own[index + 1], ahead_part, behind_part)))
        sent_kept, sent_passed, kept, passed = spread(
            term_order,
            after(mixed, *passed_before),
            (out_own[index], ahead, near, back, behind),
            "spread_%d" % index,
        )
        if index:
            outputs[-1] = hold(outputs[-1], flops=5000000000)
            sent_kept = after(sent_kept, outputs[-1])
        with jax.named_scope("core_passed_%d" % index):
            passed = (passed + from_tensor(sent_passed, 1).astype(F32)).astype(BF)
        with jax.named_scope("z_sum_%d" % index):
            arrived = from_tensor(passed, 2)
        with jax.named_scope("core_kept_%d" % index):
            kept = kept + from_tensor(sent_kept, 1).astype(F32)
        passed_before = [passed]
        base = residual[:, low:high].astype(F32)
        outputs.append((base + (kept + arrived.astype(F32))).astype(BF))
    result = jnp.concatenate(outputs, axis=1)
    return (result[:rows][None], stashed[None], result[rows:][None])


def solution(mesh):
    return jax.shard_map(
        body,
        mesh=mesh,
        in_specs=(
            P("section", "ctx", "tensor"),
            P("section", "ctx", "tensor"),
            P("section", "ctx"),
            P("section", "ctx"),
            P("section", None),
            P("section", "ctx", "tensor"),
            P("section", "ctx", "tensor"),
            P("section", "ctx", "tensor"),
            P("section", "tensor", "ctx"),
        ),
        out_specs=(
            P("section", "ctx", "tensor"),
            P("section", "ctx", "tensor"),
            P("section", "ctx", "tensor"),
        ),
        check_vma=False,
    )
```

```python
import functools
import math

import jax
import jax.numpy as jnp
from jax import lax
from jax.experimental import pallas as pl
from jax.experimental.pallas import tpu as pltpu
from jax.sharding import PartitionSpec as P

HEAD = 128
norm_epsilon = 1e-05
rope_base = 500000.0
BF = jnp.bfloat16
F32 = jnp.float32
STRIPS = (5, 3)
SHORT = 10**10
LONG = 4 * 10**10


def after(value, *earlier):
    return lax.optimization_barrier((value,) + earlier)[0]


def hold_kernel(*refs):
    del refs


def hold(value, *earlier, flops):
    anywhere = pl.BlockSpec(memory_space=pl.ANY)
    return pl.pallas_call(
        hold_kernel,
        in_specs=[anywhere] * (1 + len(earlier)),
        out_specs=anywhere,
        out_shape=jax.ShapeDtypeStruct(value.shape, value.dtype),
        input_output_aliases={0: 0},
        cost_estimate=pl.CostEstimate(flops=flops, transcendentals=0, bytes_accessed=1024),
        name="hold",
    )(value, *earlier)


def z_route(step, sections, tensors):
    low_count = 4
    rows = sections // low_count
    cores = 2
    high_count = tensors // cores
    depth = low_count * high_count
    route = []
    for z in range(depth):
        origin = (z + step) % depth
        for y in range(rows):
            for core in range(cores):
                source = ((origin % low_count) * rows + y) * tensors + (origin // low_count) * cores + core
                target = ((z % low_count) * rows + y) * tensors + (z // low_count) * cores + core
                route.append((source, target))
    return route


def from_z(block, step):
    route = z_route(step, lax.axis_size("section"), lax.axis_size("tensor"))
    return lax.ppermute(block, ("section", "tensor"), route)


def from_x(block, step):
    count = lax.axis_size("ctx")
    return lax.ppermute(block, "ctx", [((c + step) % count, c) for c in range(count)])


def from_before(block, step):
    count = lax.axis_size("ctx")
    return lax.ppermute(block, "ctx", [(c - step, c) for c in range(step, count)])


def from_tensor(block, flip):
    count = lax.axis_size("tensor")
    return lax.ppermute(block, "tensor", [(t, t ^ flip) for t in range(count)])


def first_hop(shard):
    return from_x(shard, 1), from_x(shard, -1)


def second_hop(ahead, behind):
    half = ahead.shape[0] // 2
    return from_x(ahead[:half], 1), from_x(behind[half:], -1)


def rope_tables(rows):
    half = HEAD // 2
    exponent = jnp.arange(half).astype(F32) * (2.0 / HEAD)
    inverse = jnp.exp(-exponent * math.log(rope_base))
    positions = lax.axis_index("ctx") * rows + jnp.arange(rows, dtype=jnp.int32)
    angles = positions.astype(F32)[:, None] * inverse[None, :]
    cosine = jnp.cos(angles)
    sine = jnp.sin(angles)
    return jnp.concatenate((cosine, cosine), axis=1), jnp.concatenate((-sine, sine), axis=1)


def normalize_kernel(*refs):
    block_refs, gain_ref, out_ref = refs[:8], refs[8], refs[9]
    for batch in range(2):
        blocks = [ref[...].astype(F32) for ref in block_refs[4 * batch : 4 * batch + 4]]
        total = sum(jnp.sum(block * block, axis=1, keepdims=True) for block in blocks)
        scale = lax.rsqrt(total * (1.0 / (blocks[0].shape[1] * len(blocks))) + norm_epsilon)
        for flip, block in enumerate(blocks):
            gain = gain_ref[flip : flip + 1].astype(F32)
            out_ref[flip, batch] = (block * scale * gain).astype(BF)


def normalize(blocks, gains, rows):
    width = gains.shape[1]
    step = 64
    split = [
        pl.BlockSpec((step, width), functools.partial(lambda skip, n: (skip + n, 0), part * (rows // step)))
        for _, part in blocks
    ]
    out = pl.pallas_call(
        normalize_kernel,
        grid=(rows // step,),
        in_specs=split + [pl.BlockSpec(gains.shape, lambda n: (0, 0))],
        out_specs=pl.BlockSpec((4, 2, step, width), lambda n: (0, 0, n, 0)),
        out_shape=jax.ShapeDtypeStruct((4, 2, rows, width), BF),
        compiler_params=pltpu.CompilerParams(vmem_limit_bytes=24 << 20),
        cost_estimate=pl.CostEstimate(flops=1024, transcendentals=0, bytes_accessed=1024),
        name="normalize",
    )(*[array for array, _ in blocks], gains)
    return out.reshape(4, 2 * rows, width)


def project_kernel(index_ref, normed_ref, *refs, pieces, turned):
    piece_refs, (cosine_ref, sine_ref, out_ref) = refs[: len(pieces)], refs[len(pieces) :]
    total = sum(
        jnp.dot(
            normed_ref[index_ref[step], :, low : low + ref.shape[0]], ref[...], preferred_element_type=F32
        )
        for (step, low), ref in zip(pieces, piece_refs)
    )
    for head in range(total.shape[1] // HEAD):
        raw = total[:, head * HEAD : (head + 1) * HEAD]
        if head < turned:
            raw = raw * cosine_ref[...] + pltpu.roll(raw, HEAD // 2, 1) * sine_ref[...]
        out_ref[:, head * HEAD : (head + 1) * HEAD] = raw.astype(BF)


def project(order, normed, shards, cosine, sine, turned, name):
    blocks, tokens, depth = normed.shape
    arrays = [array for array, _, _ in shards]
    columns = arrays[0].shape[1]
    wide = 2 * HEAD
    whole = lambda n, order: (0, 0)
    strip = lambda n, order: (0, n)
    return pl.pallas_call(
        functools.partial(project_kernel, pieces=[(step, low) for _, step, low in shards], turned=turned),
        grid_spec=pltpu.PrefetchScalarGridSpec(
            num_scalar_prefetch=1,
            grid=(columns // wide,),
            in_specs=[pl.BlockSpec((blocks, tokens, depth), lambda n, order: (0, 0, 0))]
            + [pl.BlockSpec((array.shape[0], wide), strip) for array in arrays]
            + [pl.BlockSpec((tokens, HEAD), whole)] * 2,
            out_specs=pl.BlockSpec((tokens, wide), strip),
        ),
        out_shape=jax.ShapeDtypeStruct((tokens, columns), BF),
        compiler_params=pltpu.CompilerParams(vmem_limit_bytes=32 << 20),
        cost_estimate=pl.CostEstimate(flops=1024, transcendentals=0, bytes_accessed=1024),
        name=name,
    )(order, normed, *arrays, cosine, sine)


def attend_kernel(
    place_ref, query_ref, query_doc_ref, two_ref, one_ref, own_ref, out_ref, bias_ref, key_scratch, value_scratch
):
    rows, span = bias_ref.shape
    back = span - rows

    @pl.when(pl.program_id(1) == 0)
    def _():
        at_query = lax.broadcasted_iota(jnp.int32, (rows, rows), 0)
        at_key = lax.broadcasted_iota(jnp.int32, (rows, rows), 1)
        query_docs = query_doc_ref[0]
        for part, ref in enumerate((two_ref, one_ref, own_ref)):
            place = slice(part * rows, (part + 1) * rows)
            first = ref.shape[1] - rows
            key_scratch[place] = ref[0, first:, :HEAD]
            value_scratch[place] = ref[0, first:, HEAD:]
            exists = place_ref[0] >= 2 - part
            key_docs = jnp.where(exists, ref[0, 0:1, :].astype(F32), -1.0)
            allowed = (at_key + (part * rows - back) <= at_query) & (query_docs == key_docs)
            bias_ref[:, place] = jnp.where(allowed, 0.0, -jnp.inf)

    for head in range(query_ref.shape[1] // HEAD):
        part = slice(head * HEAD, (head + 1) * HEAD)
        scores = lax.dot_general(
            query_ref[:, part], key_scratch[...], (((1,), (1,)), ((), ())), preferred_element_type=F32
        )
        masked = scores + bias_ref[...]
        peak = jnp.max(masked, axis=1, keepdims=True)
        weights = jnp.exp((masked - peak) * (1.0 / math.sqrt(HEAD)))
        totals = jnp.sum(weights, axis=1, keepdims=True)
        mixed = jnp.dot(weights.astype(BF), value_scratch[...], preferred_element_type=F32)
        out_ref[:, part] = (mixed / totals).astype(BF)


def attend(place, queries, query_docs, two, one, own):
    batches, rows, _ = query_docs.shape
    span = 3 * rows
    wide = 2 * HEAD
    pair = pl.BlockSpec((1,) + own.shape[1:], lambda b, h: (b, 0, 0))
    return pl.pallas_call(
        attend_kernel,
        grid=(batches, queries.shape[1] // wide),
        in_specs=[
            pl.BlockSpec(memory_space=pltpu.SMEM),
            pl.BlockSpec((rows, wide), lambda b, h: (b, h)),
            pl.BlockSpec((1, rows, 1), lambda b, h: (b, 0, 0)),
            pair,
            pair,
            pair,
        ],
        out_specs=pl.BlockSpec((rows, wide), lambda b, h: (b, h)),
        out_shape=jax.ShapeDtypeStruct(queries.shape, BF),
        scratch_shapes=[pltpu.VMEM((rows, span), F32), pltpu.VMEM((span, HEAD), BF), pltpu.VMEM((span, HEAD), BF)],
        compiler_params=pltpu.CompilerParams(vmem_limit_bytes=24 << 20),
        cost_estimate=pl.CostEstimate(flops=1024, transcendentals=0, bytes_accessed=1024),
        name="attend",
    )(place, queries, query_docs, two, one, own)


def spread_kernel(
    index_ref, mixed_ref, own_ref, ahead_ref, near_ref, back_ref, behind_ref,
    sent_kept_ref, sent_passed_ref, kept_ref, passed_ref, terms_ref,
):
    half = near_ref.shape[0]
    for step, shard in ((0, own_ref), (1, ahead_ref), (3, behind_ref)):
        terms_ref[step] = jnp.dot(mixed_ref[...], shard[...], preferred_element_type=F32)
    terms_ref[2] = jnp.dot(mixed_ref[:, :half], near_ref[...], preferred_element_type=F32) + jnp.dot(
        mixed_ref[:, half:], back_ref[...], preferred_element_type=F32
    )
    sent_kept_ref[...] = terms_ref[index_ref[1]].astype(BF)
    sent_passed_ref[...] = terms_ref[index_ref[3]].astype(BF)
    kept_ref[...] = terms_ref[index_ref[0]]
    passed_ref[...] = terms_ref[index_ref[2]]


def spread(order, mixed, shards, name):
    tokens, _ = mixed.shape
    columns = shards[0].shape[1]
    return pl.pallas_call(
        spread_kernel,
        in_specs=[pl.BlockSpec(memory_space=pltpu.SMEM)] + [pl.BlockSpec(memory_space=pltpu.VMEM)] * 6,
        out_specs=[pl.BlockSpec(memory_space=pltpu.VMEM)] * 4,
        out_shape=[
            jax.ShapeDtypeStruct((tokens, columns), BF),
            jax.ShapeDtypeStruct((tokens, columns), BF),
            jax.ShapeDtypeStruct((tokens, columns), F32),
            jax.ShapeDtypeStruct((tokens, columns), F32),
        ],
        scratch_shapes=[pltpu.VMEM((4, tokens, columns), F32)],
        compiler_params=pltpu.CompilerParams(vmem_limit_bytes=24 << 20),
        cost_estimate=pl.CostEstimate(flops=1024, transcendentals=0, bytes_accessed=1024),
        name=name,
    )(order, mixed, *shards)


def body(
    arriving,
    stored,
    docs_forward,
    docs_backward,
    norm_gain,
    query_weight,
    key_weight,
    value_projection_weight,
    out_weight,
):
    mine = arriving[0]
    held = stored[0]
    rows, width = mine.shape
    ring = lax.axis_size("ctx")
    c = lax.axis_index("ctx")
    t = lax.axis_index("tensor")
    near_high = lax.axis_index("section") < lax.axis_size("section") // 2
    docs = jnp.stack((docs_forward[0], docs_backward[0]), axis=0)
    flips = jnp.arange(4, dtype=jnp.int32)
    half = rows // 2

    strips = []
    start = 0
    for share in STRIPS:
        strips.append((start, start + width * share // sum(STRIPS)))
        start = strips[-1][1]
    out_own = [out_weight[0][:, low:high] for low, high in strips]

    q_weight = query_weight[0]
    depth = q_weight.shape[0] // 2
    with jax.named_scope("q_hop1"):
        q_ahead, q_behind = first_hop(q_weight)
    kv_weight = jnp.concatenate((key_weight[0], value_projection_weight[0]), axis=1)
    with jax.named_scope("kv_hop1"):
        kv_ahead, kv_behind = first_hop(after(kv_weight, q_ahead, q_behind))
    both = jnp.concatenate((mine, held), axis=0)
    with jax.named_scope("z_in"):
        up, down = from_z(both, 2), from_z(both, -2)
        up = hold(up, down, flops=SHORT)
    stashed = jnp.where(near_high, up[:rows], down[:rows])
    fetched = jnp.where(near_high, up[rows:], down[rows:])
    fetched_far = jnp.where(near_high, down[rows:], up[rows:])
    q_low, q_high = q_ahead[:depth], q_behind[depth:]
    far_up, far_down = up[:half], down[half:rows]
    q_low, q_high, far_up, far_down, kv_ahead, kv_behind, fetched, fetched_far, out_own[0] = lax.optimization_barrier(
        (q_low, q_high, far_up, far_down, kv_ahead, kv_behind, fetched, fetched_far, out_own[0])
    )

    with jax.named_scope("q_hop2"):
        across_low, across_high = from_x(q_low, 1), from_x(q_high, -1)
    with jax.named_scope("kv_hop2"):
        kv_near, kv_back = second_hop(kv_ahead, kv_behind)
    with jax.named_scope("far"):
        mine_far = jnp.concatenate((from_z(far_up, 2), from_z(far_down, -2)), axis=0)
    with jax.named_scope("sib"):
        sib = from_tensor(jnp.concatenate((mine, fetched, fetched_far, mine_far), axis=0), 1)
    blocks = (
        ((mine, 0), (sib, 0), (mine_far, 0), (sib, 3))
        + ((fetched, 0), (sib, 1), (fetched_far, 0), (sib, 2))
    )
    gains = norm_gain[0].reshape(-1, width)
    normed = normalize(blocks, jnp.take(gains, t ^ flips, axis=0), rows)
    cosine, sine = rope_tables(rows)
    cosine, sine = jnp.concatenate((cosine, cosine), axis=0), jnp.concatenate((sine, sine), axis=0)
    feature_order = t ^ ((c + flips) % ring)

    own_kv = project(
        feature_order,
        normed,
        ((kv_weight, 0, 0), (kv_ahead, 1, 0), (kv_near, 2, 0), (kv_back, 2, depth), (kv_behind, 3, 0)),
        cosine,
        sine,
        1,
        "project_kv",
    )
    id_rows = 16
    ids = jnp.broadcast_to(docs.astype(BF)[:, None, :], (2, id_rows, rows))
    own_pair = jnp.concatenate((ids, own_kv.reshape(2, rows, 2 * HEAD)), axis=1)
    with jax.named_scope("kv_rows"):
        kv_one, kv_two = from_before(own_pair, 1), from_before(own_pair, 2)
    with jax.named_scope("out_hop1_0"):
        out_own[0] = hold(out_own[0], across_low, across_high, kv_near, kv_back, flops=LONG)
        out_hops = [first_hop(out_own[0])]
    queries = project(
        feature_order,
        after(normed, own_kv),
        (
            (q_weight, 0, 0),
            (q_ahead, 1, 0),
            (q_behind, 3, 0),
            (across_low, 2, 0),
            (across_high, 2, depth),
        ),
        cosine,
        sine,
        2,
        "project_q",
    )
    queries, out_own[1] = lax.optimization_barrier((queries, out_own[1]))
    kv_one = hold(kv_one, kv_two, queries, flops=SHORT)
    mixed = attend(c.reshape(1), queries, docs.astype(F32)[:, :, None], kv_two, kv_one, own_pair)

    residual = jnp.concatenate((mine, fetched), axis=0)
    term_order = ((t ^ flips) - c) % ring
    passed_before = []
    outputs = []
    for index, (low, high) in enumerate(strips):
        ahead, behind = out_hops[index]
        with jax.named_scope("out_hop2_%d" % index):
            near, back = second_hop(ahead, behind)
        if index + 1 < len(strips):
            with jax.named_scope("out_hop1_%d" % (index + 1)):
                out_hops.append(first_hop(after(out_own[index + 1], near, back)))
        sent_kept, sent_passed, kept, passed = spread(
            term_order,
            after(mixed, *passed_before),
            (out_own[index], ahead, near, back, behind),
            "spread_%d" % index,
        )
        if index:
            sent_passed = after(sent_passed, outputs[-1])
        with jax.named_scope("core_passed_%d" % index):
            passed = (passed + from_tensor(sent_passed, 1).astype(F32)).astype(BF)
        with jax.named_scope("z_sum_%d" % index):
            arrived = from_tensor(passed, 2)
        with jax.named_scope("core_kept_%d" % index):
            kept = kept + from_tensor(sent_kept, 1).astype(F32)
        passed_before = [passed]
        base = residual[:, low:high].astype(F32)
        outputs.append((base + (kept + arrived.astype(F32))).astype(BF))
    result = jnp.concatenate(outputs, axis=1)
    return (result[:rows][None], stashed[None], result[rows:][None])


def solution(mesh):
    return jax.shard_map(
        body,
        mesh=mesh,
        in_specs=(
            P("section", "ctx", "tensor"),
            P("section", "ctx", "tensor"),
            P("section", "ctx"),
            P("section", "ctx"),
            P("section", None),
            P("section", "ctx", "tensor"),
            P("section", "ctx", "tensor"),
            P("section", "ctx", "tensor"),
            P("section", "tensor", "ctx"),
        ),
        out_specs=(
            P("section", "ctx", "tensor"),
            P("section", "ctx", "tensor"),
            P("section", "ctx", "tensor"),
        ),
        check_vma=False,
    )
```

```python
import functools
import math

import jax
import jax.numpy as jnp
from jax import lax
from jax.experimental import pallas as pl
from jax.experimental.pallas import tpu as pltpu
from jax.sharding import PartitionSpec as P

HEAD = 128
norm_epsilon = 1e-05
rope_base = 500000.0
BF = jnp.bfloat16
F32 = jnp.float32
STRIPS = (5, 3)
SHORT = 10**10
LONG = 4 * 10**10


def after(value, *earlier):
    return lax.optimization_barrier((value,) + earlier)[0]


def hold_kernel(*refs):
    del refs


def hold(value, *earlier, flops):
    anywhere = pl.BlockSpec(memory_space=pl.ANY)
    return pl.pallas_call(
        hold_kernel,
        in_specs=[anywhere] * (1 + len(earlier)),
        out_specs=anywhere,
        out_shape=jax.ShapeDtypeStruct(value.shape, value.dtype),
        input_output_aliases={0: 0},
        cost_estimate=pl.CostEstimate(flops=flops, transcendentals=0, bytes_accessed=1024),
        name="hold",
    )(value, *earlier)


def z_route(step, sections, tensors):
    low_count = 4
    rows = sections // low_count
    cores = 2
    high_count = tensors // cores
    depth = low_count * high_count
    route = []
    for z in range(depth):
        origin = (z + step) % depth
        for y in range(rows):
            for core in range(cores):
                source = ((origin % low_count) * rows + y) * tensors + (origin // low_count) * cores + core
                target = ((z % low_count) * rows + y) * tensors + (z // low_count) * cores + core
                route.append((source, target))
    return route


def from_z(block, step):
    route = z_route(step, lax.axis_size("section"), lax.axis_size("tensor"))
    return lax.ppermute(block, ("section", "tensor"), route)


def from_x(block, step):
    count = lax.axis_size("ctx")
    return lax.ppermute(block, "ctx", [((c + step) % count, c) for c in range(count)])


def from_before(block, step):
    count = lax.axis_size("ctx")
    return lax.ppermute(block, "ctx", [(c - step, c) for c in range(step, count)])


def from_tensor(block, flip):
    count = lax.axis_size("tensor")
    return lax.ppermute(block, "tensor", [(t, t ^ flip) for t in range(count)])


def first_hop(shard):
    return from_x(shard, 1), from_x(shard, -1)


def second_hop(ahead, behind):
    half = ahead.shape[0] // 2
    return from_x(ahead[:half], 1), from_x(behind[half:], -1)


def rope_tables(rows):
    half = HEAD // 2
    exponent = jnp.arange(half).astype(F32) * (2.0 / HEAD)
    inverse = jnp.exp(-exponent * math.log(rope_base))
    positions = lax.axis_index("ctx") * rows + jnp.arange(rows, dtype=jnp.int32)
    angles = positions.astype(F32)[:, None] * inverse[None, :]
    cosine = jnp.cos(angles)
    sine = jnp.sin(angles)
    return jnp.concatenate((cosine, cosine), axis=1), jnp.concatenate((-sine, sine), axis=1)


def normalize_kernel(*refs):
    block_refs, gain_ref, out_ref = refs[:8], refs[8], refs[9]
    for batch in range(2):
        blocks = [ref[...].astype(F32) for ref in block_refs[4 * batch : 4 * batch + 4]]
        total = sum(jnp.sum(block * block, axis=1, keepdims=True) for block in blocks)
        scale = lax.rsqrt(total * (1.0 / (blocks[0].shape[1] * len(blocks))) + norm_epsilon)
        for flip, block in enumerate(blocks):
            gain = gain_ref[flip : flip + 1].astype(F32)
            out_ref[flip, batch] = (block * scale * gain).astype(BF)


def normalize(blocks, gains, rows):
    width = gains.shape[1]
    step = 64
    split = [
        pl.BlockSpec((step, width), functools.partial(lambda skip, n: (skip + n, 0), part * (rows // step)))
        for _, part in blocks
    ]
    out = pl.pallas_call(
        normalize_kernel,
        grid=(rows // step,),
        in_specs=split + [pl.BlockSpec(gains.shape, lambda n: (0, 0))],
        out_specs=pl.BlockSpec((4, 2, step, width), lambda n: (0, 0, n, 0)),
        out_shape=jax.ShapeDtypeStruct((4, 2, rows, width), BF),
        compiler_params=pltpu.CompilerParams(vmem_limit_bytes=24 << 20),
        cost_estimate=pl.CostEstimate(flops=1024, transcendentals=0, bytes_accessed=1024),
        name="normalize",
    )(*[array for array, _ in blocks], gains)
    return out.reshape(4, 2 * rows, width)


def project_kernel(index_ref, normed_ref, *refs, pieces, turned):
    piece_refs, (cosine_ref, sine_ref, out_ref) = refs[: len(pieces)], refs[len(pieces) :]
    total = sum(
        jnp.dot(
            normed_ref[index_ref[step], :, low : low + ref.shape[0]], ref[...], preferred_element_type=F32
        )
        for (step, low), ref in zip(pieces, piece_refs)
    )
    for head in range(total.shape[1] // HEAD):
        raw = total[:, head * HEAD : (head + 1) * HEAD]
        if head < turned:
            raw = raw * cosine_ref[...] + pltpu.roll(raw, HEAD // 2, 1) * sine_ref[...]
        out_ref[:, head * HEAD : (head + 1) * HEAD] = raw.astype(BF)


def project(order, normed, shards, cosine, sine, turned, name):
    blocks, tokens, depth = normed.shape
    arrays = [array for array, _, _ in shards]
    columns = arrays[0].shape[1]
    wide = 2 * HEAD
    whole = lambda n, order: (0, 0)
    strip = lambda n, order: (0, n)
    return pl.pallas_call(
        functools.partial(project_kernel, pieces=[(step, low) for _, step, low in shards], turned=turned),
        grid_spec=pltpu.PrefetchScalarGridSpec(
            num_scalar_prefetch=1,
            grid=(columns // wide,),
            in_specs=[pl.BlockSpec((blocks, tokens, depth), lambda n, order: (0, 0, 0))]
            + [pl.BlockSpec((array.shape[0], wide), strip) for array in arrays]
            + [pl.BlockSpec((tokens, HEAD), whole)] * 2,
            out_specs=pl.BlockSpec((tokens, wide), strip),
        ),
        out_shape=jax.ShapeDtypeStruct((tokens, columns), BF),
        compiler_params=pltpu.CompilerParams(vmem_limit_bytes=32 << 20),
        cost_estimate=pl.CostEstimate(flops=1024, transcendentals=0, bytes_accessed=1024),
        name=name,
    )(order, normed, *arrays, cosine, sine)


def attend_kernel(
    place_ref, query_ref, query_doc_ref, two_ref, one_ref, own_ref, out_ref, bias_ref, key_scratch, value_scratch
):
    rows, span = bias_ref.shape
    back = span - rows

    @pl.when(pl.program_id(1) == 0)
    def _():
        at_query = lax.broadcasted_iota(jnp.int32, (rows, rows), 0)
        at_key = lax.broadcasted_iota(jnp.int32, (rows, rows), 1)
        query_docs = query_doc_ref[0]
        for part, ref in enumerate((two_ref, one_ref, own_ref)):
            place = slice(part * rows, (part + 1) * rows)
            first = ref.shape[1] - rows
            key_scratch[place] = ref[0, first:, :HEAD]
            value_scratch[place] = ref[0, first:, HEAD:]
            exists = place_ref[0] >= 2 - part
            key_docs = jnp.where(exists, ref[0, 0:1, :].astype(F32), -1.0)
            allowed = (at_key + (part * rows - back) <= at_query) & (query_docs == key_docs)
            bias_ref[:, place] = jnp.where(allowed, 0.0, -jnp.inf)

    for head in range(query_ref.shape[1] // HEAD):
        part = slice(head * HEAD, (head + 1) * HEAD)
        scores = lax.dot_general(
            query_ref[:, part], key_scratch[...], (((1,), (1,)), ((), ())), preferred_element_type=F32
        )
        masked = scores + bias_ref[...]
        peak = jnp.max(masked, axis=1, keepdims=True)
        weights = jnp.exp((masked - peak) * (1.0 / math.sqrt(HEAD)))
        totals = jnp.sum(weights, axis=1, keepdims=True)
        mixed = jnp.dot(weights.astype(BF), value_scratch[...], preferred_element_type=F32)
        out_ref[:, part] = (mixed / totals).astype(BF)


def attend(place, queries, query_docs, two, one, own):
    batches, rows, _ = query_docs.shape
    span = 3 * rows
    wide = 2 * HEAD
    pair = pl.BlockSpec((1,) + own.shape[1:], lambda b, h: (b, 0, 0))
    return pl.pallas_call(
        attend_kernel,
        grid=(batches, queries.shape[1] // wide),
        in_specs=[
            pl.BlockSpec(memory_space=pltpu.SMEM),
            pl.BlockSpec((rows, wide), lambda b, h: (b, h)),
            pl.BlockSpec((1, rows, 1), lambda b, h: (b, 0, 0)),
            pair,
            pair,
            pair,
        ],
        out_specs=pl.BlockSpec((rows, wide), lambda b, h: (b, h)),
        out_shape=jax.ShapeDtypeStruct(queries.shape, BF),
        scratch_shapes=[pltpu.VMEM((rows, span), F32), pltpu.VMEM((span, HEAD), BF), pltpu.VMEM((span, HEAD), BF)],
        compiler_params=pltpu.CompilerParams(vmem_limit_bytes=24 << 20),
        cost_estimate=pl.CostEstimate(flops=1024, transcendentals=0, bytes_accessed=1024),
        name="attend",
    )(place, queries, query_docs, two, one, own)


def spread_kernel(
    index_ref, mixed_ref, own_ref, ahead_ref, near_ref, back_ref, behind_ref,
    sent_kept_ref, sent_passed_ref, kept_ref, passed_ref, terms_ref,
):
    half = near_ref.shape[0]
    for step, shard in ((0, own_ref), (1, ahead_ref), (3, behind_ref)):
        terms_ref[step] = jnp.dot(mixed_ref[...], shard[...], preferred_element_type=F32)
    terms_ref[2] = jnp.dot(mixed_ref[:, :half], near_ref[...], preferred_element_type=F32) + jnp.dot(
        mixed_ref[:, half:], back_ref[...], preferred_element_type=F32
    )
    sent_kept_ref[...] = terms_ref[index_ref[1]].astype(BF)
    sent_passed_ref[...] = terms_ref[index_ref[3]].astype(BF)
    kept_ref[...] = terms_ref[index_ref[0]]
    passed_ref[...] = terms_ref[index_ref[2]]


def spread(order, mixed, shards, name):
    tokens, _ = mixed.shape
    columns = shards[0].shape[1]
    return pl.pallas_call(
        spread_kernel,
        in_specs=[pl.BlockSpec(memory_space=pltpu.SMEM)] + [pl.BlockSpec(memory_space=pltpu.VMEM)] * 6,
        out_specs=[pl.BlockSpec(memory_space=pltpu.VMEM)] * 4,
        out_shape=[
            jax.ShapeDtypeStruct((tokens, columns), BF),
            jax.ShapeDtypeStruct((tokens, columns), BF),
            jax.ShapeDtypeStruct((tokens, columns), F32),
            jax.ShapeDtypeStruct((tokens, columns), F32),
        ],
        scratch_shapes=[pltpu.VMEM((4, tokens, columns), F32)],
        compiler_params=pltpu.CompilerParams(vmem_limit_bytes=24 << 20),
        cost_estimate=pl.CostEstimate(flops=1024, transcendentals=0, bytes_accessed=1024),
        name=name,
    )(order, mixed, *shards)


def body(
    arriving,
    stored,
    docs_forward,
    docs_backward,
    norm_gain,
    query_weight,
    key_weight,
    value_projection_weight,
    out_weight,
):
    mine = arriving[0]
    held = stored[0]
    rows, width = mine.shape
    ring = lax.axis_size("ctx")
    c = lax.axis_index("ctx")
    t = lax.axis_index("tensor")
    near_high = lax.axis_index("section") < lax.axis_size("section") // 2
    docs = jnp.stack((docs_forward[0], docs_backward[0]), axis=0)
    flips = jnp.arange(4, dtype=jnp.int32)
    half = rows // 2

    strips = []
    start = 0
    for share in STRIPS:
        strips.append((start, start + width * share // sum(STRIPS)))
        start = strips[-1][1]
    out_own = [out_weight[0][:, low:high] for low, high in strips]

    q_weight = query_weight[0]
    depth = q_weight.shape[0] // 2
    with jax.named_scope("q_hop1"):
        q_ahead, q_behind = first_hop(q_weight)
    kv_weight = jnp.concatenate((key_weight[0], value_projection_weight[0]), axis=1)
    with jax.named_scope("kv_hop1"):
        kv_ahead, kv_behind = first_hop(after(kv_weight, q_ahead, q_behind))
    both = jnp.concatenate((mine, held), axis=0)
    with jax.named_scope("z_in"):
        up, down = from_z(both, 2), from_z(both, -2)
        up = hold(up, down, flops=SHORT)
    q_low, q_high = q_ahead[:depth], q_behind[depth:]
    far_up, far_down = up[:half], down[half:rows]
    q_low, q_high, far_up, far_down, kv_ahead, kv_behind, up, down, out_own[0] = lax.optimization_barrier(
        (q_low, q_high, far_up, far_down, kv_ahead, kv_behind, up, down, out_own[0])
    )
    stashed = jnp.where(near_high, up[:rows], down[:rows])
    fetched = jnp.where(near_high, up[rows:], down[rows:])
    fetched_far = jnp.where(near_high, down[rows:], up[rows:])

    with jax.named_scope("q_hop2"):
        across_low, across_high = from_x(q_low, 1), from_x(q_high, -1)
    with jax.named_scope("kv_hop2"):
        kv_near, kv_back = second_hop(kv_ahead, kv_behind)
    with jax.named_scope("far"):
        mine_far = jnp.concatenate((from_z(far_up, 2), from_z(far_down, -2)), axis=0)
    with jax.named_scope("sib"):
        sib = from_tensor(jnp.concatenate((mine, fetched, fetched_far, mine_far), axis=0), 1)
    blocks = (
        ((mine, 0), (sib, 0), (mine_far, 0), (sib, 3))
        + ((fetched, 0), (sib, 1), (fetched_far, 0), (sib, 2))
    )
    gains = norm_gain[0].reshape(-1, width)
    normed = normalize(blocks, jnp.take(gains, t ^ flips, axis=0), rows)
    cosine, sine = rope_tables(rows)
    cosine, sine = jnp.concatenate((cosine, cosine), axis=0), jnp.concatenate((sine, sine), axis=0)
    feature_order = t ^ ((c + flips) % ring)

    own_kv = project(
        feature_order,
        normed,
        ((kv_weight, 0, 0), (kv_ahead, 1, 0), (kv_near, 2, 0), (kv_back, 2, depth), (kv_behind, 3, 0)),
        cosine,
        sine,
        1,
        "project_kv",
    )
    id_rows = 16
    ids = jnp.broadcast_to(docs.astype(BF)[:, None, :], (2, id_rows, rows))
    own_pair = jnp.concatenate((ids, own_kv.reshape(2, rows, 2 * HEAD)), axis=1)
    with jax.named_scope("kv_rows"):
        kv_one, kv_two = from_before(own_pair, 1), from_before(own_pair, 2)
    with jax.named_scope("out_hop1_0"):
        out_own[0] = hold(out_own[0], across_low, across_high, kv_near, kv_back, flops=LONG)
        out_hops = [first_hop(out_own[0])]
    queries = project(
        feature_order,
        after(normed, own_kv),
        (
            (q_weight, 0, 0),
            (q_ahead, 1, 0),
            (q_behind, 3, 0),
            (across_low, 2, 0),
            (across_high, 2, depth),
        ),
        cosine,
        sine,
        2,
        "project_q",
    )
    queries, out_own[1] = lax.optimization_barrier((queries, out_own[1]))
    kv_one = hold(kv_one, kv_two, queries, flops=SHORT)
    mixed = attend(c.reshape(1), queries, docs.astype(F32)[:, :, None], kv_two, kv_one, own_pair)

    residual = jnp.concatenate((mine, fetched), axis=0)
    term_order = ((t ^ flips) - c) % ring
    passed_before = []
    outputs = []
    for index, (low, high) in enumerate(strips):
        ahead, behind = out_hops[index]
        with jax.named_scope("out_hop2_%d" % index):
            near, back = second_hop(ahead, behind)
        if index + 1 < len(strips):
            with jax.named_scope("out_hop1_%d" % (index + 1)):
                out_hops.append(first_hop(after(out_own[index + 1], near, back)))
        sent_kept, sent_passed, kept, passed = spread(
            term_order,
            after(mixed, *passed_before),
            (out_own[index], ahead, near, back, behind),
            "spread_%d" % index,
        )
        if index:
            sent_passed = after(sent_passed, outputs[-1])
        with jax.named_scope("core_passed_%d" % index):
            passed = (passed + from_tensor(sent_passed, 1).astype(F32)).astype(BF)
        with jax.named_scope("z_sum_%d" % index):
            arrived = from_tensor(passed, 2)
        with jax.named_scope("core_kept_%d" % index):
            kept = kept + from_tensor(sent_kept, 1).astype(F32)
        passed_before = [passed]
        base = residual[:, low:high].astype(F32)
        outputs.append((base + (kept + arrived.astype(F32))).astype(BF))
    result = jnp.concatenate(outputs, axis=1)
    return (result[:rows][None], stashed[None], result[rows:][None])


def solution(mesh):
    return jax.shard_map(
        body,
        mesh=mesh,
        in_specs=(
            P("section", "ctx", "tensor"),
            P("section", "ctx", "tensor"),
            P("section", "ctx"),
            P("section", "ctx"),
            P("section", None),
            P("section", "ctx", "tensor"),
            P("section", "ctx", "tensor"),
            P("section", "ctx", "tensor"),
            P("section", "tensor", "ctx"),
        ),
        out_specs=(
            P("section", "ctx", "tensor"),
            P("section", "ctx", "tensor"),
            P("section", "ctx", "tensor"),
        ),
        check_vma=False,
    )
```
